128 devices in a mesh: re: 32 (over y, x, z_lo), rp: 4 (over z_hi, core).
Axes of the slice: x: 4, y: 4, z: 4 (z_hi: 2, z_lo: 2; z = z_hi * 2 + z_lo), core: 2. Of those that a mesh axis runs over, the one named last changes fastest.
Arguments:
- wannier_table: bfloat16 [1024, 128, 1536], P('re', 'rp'), may hold values from -0.0078125 to 0.0078125
- mode_matrix: float32 [2, 12, 12], replicated, may hold values from -1.75 to 1.75
- re_coords: int32 [3, 1024], replicated, may hold values from -8 to 8
- rp_coords: int32 [3, 128], P(None, 'rp'), may hold values from -6 to 6
- q_coords: int32 [3, 2], replicated, may hold values from 0 to 63
- k_coords: int32 [3, 16384], P(None, 're'), may hold values from 0 to 63
- rotations: bfloat16 [16384, 128], P('re'), may hold values from -1.5 to 1.5
- kq_owner: int32 [2, 16384, 1], P(None, 're'), may hold values from 0 to 31; in each aligned block of 512 rows (0 to 511, 512 to 1023, ..., all dimensions but the last counted through in order) at most 24 rows name the same one
- kq_row: int32 [2, 16384], P(None, 're'), may hold values from 0 to 511
Outputs:
- couplings: bfloat16 [2, 12, 2, 64, 16384], P(None, 'rp', None, None, 're')
The draws below stay inside these ranges and needn't reach their ends.
Inputs may be any that keep to these rules, and one draw needn't show every extreme that they name: `kq_owner`: for each wavevector, among the 512 k-rows of one device no owner is named more than 24 times, a bound that some block reaches.
All inputs are finite; a program needn't handle non-finite values.
Results may differ from the reference program's by a relative error of at most 0.0057.
Values may be sent and summed in bfloat16 or wider, within the bound.
No kernel may reach another device: no remote copies, remote signals or barrier semaphores. Data moves between devices by JAX's collectives and lax.ppermute only.
A program may use at most 128 MiB of HBM per device.

```python
import math
import jax
import jax.numpy as jnp
import numpy as np
from jax import lax

RE = 1024
RP = 128
NB = 8
MODES = 12
Q = 2
GRID = 64
K_DEV = 512
KPTS = 16384
CAP = 24
N_RE = 32


def touch_ends(array, own_key, smallest, largest):
    spot = [jax.random.randint(jax.random.fold_in(own_key, axis), (), 0, length) for axis, length in enumerate(array.shape)]
    main_axis = array.shape.index(max(array.shape))
    next_to = spot[:main_axis] + [(spot[main_axis] + 1) % array.shape[main_axis]] + spot[main_axis + 1:]
    return array.at[tuple(spot)].set(smallest).at[tuple(next_to)].set(largest)


def steps_of(key, dims, cuts, smallest, top_value):
    gain, own = 1.0, jax.random.fold_in(key, 6)
    for dim, blocks in cuts:
        heights = jnp.exp(jax.random.uniform(jax.random.fold_in(own, dim), (blocks,), jnp.float32, smallest / len(cuts), top_value / len(cuts)))
        gain = gain * jnp.repeat(heights, dims[dim] // blocks).reshape([-1 if axis == dim else 1 for axis in range(len(dims))])
    return gain


def deal_out(rng, own, number, rows, number_of, top, limit, lean):
    order = jax.random.permutation(rng, number_of)
    crowded, common = portions_of(number_of, rows * top, limit, lean, True), portions_of(number_of, rows * top, limit, lean, False)
    places = jnp.arange(number_of)

    def named(tallies, turn):
        used = int((tallies > 0).sum())
        fixed = max(1, used // 4)
        moved = fixed + (places - fixed + turn * (used - fixed)) % max(1, number_of - fixed)
        return jnp.zeros((number_of,), jnp.int32).at[order[jnp.where(places < fixed, places, moved)]].set(jnp.asarray(tallies, jnp.int32))

    tallies = jnp.where(number % 4 == 0, named(crowded, number // 4), named(common, number - number // 4 - 1))
    mixed = jax.random.permutation(jax.random.fold_in(own, 3), number_of)
    giver, sink = mixed[0:number_of // 2 * 2:2], mixed[1:number_of // 2 * 2:2]
    slack = jnp.minimum(tallies[giver] - 1, limit - tallies[sink]) // 2
    slack = jnp.where((giver == order[0]) | (sink == order[0]) | (tallies[sink] == 0), 0, jnp.maximum(slack, 0))
    moved = jax.random.randint(jax.random.fold_in(own, 4), (number_of // 2,), 0, 1 << 20) % (slack + 1)
    tallies = tallies.at[giver].add(-moved).at[sink].add(moved)
    items = jnp.searchsorted(jnp.cumsum(tallies), jnp.arange(rows * top), side="right").astype(jnp.int32)
    listing = items.reshape(top, rows).T
    listing = listing[jax.random.permutation(jax.random.fold_in(own, 1), rows)]
    turn = jax.random.randint(jax.random.fold_in(own, 2), (rows, 1), 0, top)
    return jnp.take_along_axis(listing, (jnp.arange(top)[None, :] + turn) % top, axis=1)


def portions_of(count, total, most, slope, full):
    weights = [(1 << 20) // math.isqrt(grade ** slope) + 1 for grade in range(1, count + 1)]
    largest = most if full else min(most, max(-(-total // count), total * weights[0] // sum(weights)))
    least = 1 if total - largest >= count - 1 else 0
    counts, spare = [largest] + [least] * (count - 1), total - largest - least * (count - 1)
    while spare > 0:
        candidates = [i for i in range(1, count) if counts[i] < largest] or [i for i in range(1, count) if counts[i] < most]
        whole, budget = sum([weights[i] for i in candidates]), spare
        for i in candidates:
            more = min(most - counts[i], max(1, budget * weights[i] // whole), spare)
            counts[i] = counts[i] + more
            spare = spare - more
    return np.array(counts)


def bell_draw(rng, extent, scale, reach, split=(), kind=jnp.bfloat16):
    factor_of = steps_of(rng, extent, split, -0.22, 0.18) if split else 1.0
    entries = jax.random.normal(rng, extent, jnp.float32) * scale * factor_of
    return jnp.minimum(jnp.maximum(entries, -reach), reach).astype(kind)


def setup_inputs(seed: int = 0) -> dict:
    arg_keys = jax.random.split(jax.random.key(seed), 10)
    wannier_table = bell_draw(arg_keys[0], (RE, RP, 2 * MODES * NB * NB), (4 * RP * RE) ** -0.5, 0.0078125, ((0, 32), (1, 4)))
    mode_matrix = bell_draw(arg_keys[1], (Q, MODES, MODES), MODES ** -0.5, 1.75, (), jnp.float32)
    re_coords = touch_ends(jax.random.randint(arg_keys[2], (3, RE), -8, 9), jax.random.fold_in(arg_keys[2], 1), -8, 8).astype(jnp.int32)
    rp_coords = touch_ends(jax.random.randint(arg_keys[3], (3, RP), -6, 7), jax.random.fold_in(arg_keys[3], 1), -6, 6).astype(jnp.int32)
    q_coords = touch_ends(jax.random.randint(arg_keys[4], (3, Q), 0, GRID), jax.random.fold_in(arg_keys[4], 1), 0, GRID - 1).astype(jnp.int32)
    k_coords = touch_ends(jax.random.randint(arg_keys[5], (3, KPTS), 0, GRID), jax.random.fold_in(arg_keys[5], 1), 0, GRID - 1).astype(jnp.int32)
    rotations = bell_draw(arg_keys[6], (KPTS, 2 * NB * NB), (2 * NB) ** -0.5, 1.5, ((0, 32),))
    kq_owner_keys = jax.random.split(jax.random.fold_in(arg_keys[7], 1), Q * KPTS // K_DEV)
    kq_owner_turns = jax.random.permutation(jax.random.fold_in(arg_keys[7], 3), Q * KPTS // K_DEV)
    kq_owner = jax.vmap(lambda own, number: deal_out(jax.random.fold_in(arg_keys[7], 2), own, number, K_DEV, N_RE, 1, CAP, 1))(kq_owner_keys, kq_owner_turns).reshape((Q, KPTS, 1))
    kq_row = touch_ends(jax.random.randint(arg_keys[8], (Q, KPTS), 0, K_DEV), jax.random.fold_in(arg_keys[8], 1), 0, K_DEV - 1).astype(jnp.int32)
    return dict(wannier_table=wannier_table, mode_matrix=mode_matrix, re_coords=re_coords, rp_coords=rp_coords, q_coords=q_coords, k_coords=k_coords, rotations=rotations, kq_owner=kq_owner, kq_row=kq_row)


def phases(left, right):
    products = jnp.sum(left[:, :, None] * right[:, None, :], axis=0)
    angles = jnp.mod(products, GRID).astype(jnp.float32) * (2.0 * math.pi / GRID)
    return jnp.cos(angles).astype(jnp.bfloat16), jnp.sin(angles).astype(jnp.bfloat16)


def rotate(coupling, right_rot, left_rot):
    highest = lax.Precision.HIGHEST
    coupling_real = coupling[:, :, 0]
    coupling_imag = coupling[:, :, 1]
    right_real = right_rot[0]
    right_imag = right_rot[1]
    half_real = jnp.einsum("qvabk,bnk->qvank", coupling_real, right_real, precision=highest) - jnp.einsum("qvabk,bnk->qvank", coupling_imag, right_imag, precision=highest)
    half_imag = jnp.einsum("qvabk,bnk->qvank", coupling_real, right_imag, precision=highest) + jnp.einsum("qvabk,bnk->qvank", coupling_imag, right_real, precision=highest)
    left_real = left_rot[:, 0]
    left_imag = left_rot[:, 1]
    result_real = jnp.einsum("qamk,qvank->qvmnk", left_real, half_real, precision=highest) + jnp.einsum("qamk,qvank->qvmnk", left_imag, half_imag, precision=highest)
    result_imag = jnp.einsum("qamk,qvank->qvmnk", left_real, half_imag, precision=highest) - jnp.einsum("qamk,qvank->qvmnk", left_imag, half_real, precision=highest)
    return jnp.stack([result_real, result_imag], axis=2)


def reference(wannier_table, mode_matrix, re_coords, rp_coords, q_coords, k_coords, rotations, kq_owner, kq_row):
    highest = lax.Precision.HIGHEST
    cosine_q, sine_q = phases(q_coords, rp_coords)
    cosine_q = cosine_q.astype(jnp.float32)
    sine_q = sine_q.astype(jnp.float32)
    re_block = min(128, RE)
    width = MODES * NB * NB

    def rp_block(table_rows):
        values = table_rows.reshape(re_block, RP, 2, width).astype(jnp.float32)
        with_cos = jnp.einsum("qr,ercw->eqcw", cosine_q, values, precision=highest)
        with_sin = jnp.einsum("qr,ercw->eqcw", sine_q, values, precision=highest)
        summed = jnp.stack([with_cos[:, :, 0] - with_sin[:, :, 1], with_sin[:, :, 0] + with_cos[:, :, 1]], axis=2)
        summed = summed.reshape(re_block, Q, 2, MODES, NB * NB)
        return jnp.einsum("eqcmz,qmn->eqcnz", summed, mode_matrix, precision=highest)

    mixed = lax.map(rp_block, wannier_table.reshape(RE // re_block, re_block, RP, 2 * width))
    mixed = mixed.reshape(RE, Q, 2, width)
    coupling_q = lax.optimization_barrier(mixed.astype(jnp.bfloat16)).astype(jnp.float32)
    k_block = 512

    def one_block(block_index):
        first_row = block_index * k_block
        block_coords = lax.dynamic_slice_in_dim(k_coords, first_row, k_block, 1)
        cosine_k, sine_k = phases(re_coords, block_coords)
        cosine_k = cosine_k.astype(jnp.float32)
        sine_k = sine_k.astype(jnp.float32)
        with_cos = jnp.einsum("eqcz,ek->qczk", coupling_q, cosine_k, precision=highest)
        with_sin = jnp.einsum("eqcz,ek->qczk", coupling_q, sine_k, precision=highest)
        coupling = jnp.stack([with_cos[:, 0] - with_sin[:, 1], with_sin[:, 0] + with_cos[:, 1]], axis=1)
        coupling = coupling.reshape(Q, 2, MODES, NB, NB, k_block).transpose(0, 2, 1, 3, 4, 5)
        local_rows = lax.dynamic_slice_in_dim(rotations, first_row, k_block, 0)
        local_rot = local_rows.astype(jnp.float32).T.reshape(2, NB, NB, k_block)
        owners = lax.dynamic_slice_in_dim(kq_owner[:, :, 0], first_row, k_block, 1)
        far_rows = lax.dynamic_slice_in_dim(kq_row, first_row, k_block, 1)
        positions = (owners * K_DEV + far_rows).astype(jnp.int32)
        far_rotation = rotations[positions]
        far_rot = far_rotation.astype(jnp.float32).transpose(0, 2, 1).reshape(Q, 2, NB, NB, k_block)
        result = rotate(coupling, local_rot, far_rot)
        return result.reshape(Q, MODES, 2, NB * NB, k_block).astype(jnp.bfloat16)

    blocks = lax.map(one_block, jnp.arange(KPTS // k_block, dtype=jnp.int32))
    return blocks.transpose(1, 2, 3, 4, 0, 5).reshape(Q, MODES, 2, NB * NB, KPTS)
```

```python
import functools
import math

import jax
import jax.numpy as jnp
from jax import lax
from jax.experimental import pallas as pl
from jax.experimental.pallas import tpu as pltpu
from jax.sharding import PartitionSpec as P

NB = 8
MODES = 12
Q = 2
GRID = 64
RE = 1024
RE_LOCAL = 32
RP_LOCAL = 32
K = 512
N_RE = 32
N_RP = 4
M_LOCAL = MODES // N_RP
CAP = 24
SLOTS = Q * CAP
ROWS = Q * M_LOCAL * RE_LOCAL
PACK = ROWS + SLOTS
LANES = 128
TURN = 2.0 * math.pi
SINE = [TURN ** n * s / math.factorial(n) for n, s in ((1, 1), (3, -1), (5, 1), (7, -1), (9, 1), (11, -1))]
BF = jnp.bfloat16
F32 = jnp.float32
I32 = jnp.int32


def sine_poly(t):
    s = t * t
    value = jnp.full_like(s, SINE[-1])
    for c in SINE[-2::-1]:
        value = value * s + c
    return value * t


def cos_sin(products):
    turns = products * (1.0 / GRID)
    frac = turns - jnp.floor(turns + 0.5)
    size = jnp.abs(frac)
    shifted = 0.25 - size
    cosine = sine_poly(shifted)
    folded = 0.25 - jnp.abs(shifted)
    sine = sine_poly(jnp.where(frac < 0.0, -folded, folded))
    return cosine, sine


def requests_kernel(owner_ref, row_ref, request_ref, slot_ref):
    before = (lax.broadcasted_iota(I32, (K, K), 0) < lax.broadcasted_iota(I32, (K, K), 1)).astype(F32).astype(BF)
    total = jnp.zeros((N_RE, LANES), F32)
    for q in range(Q):
        owner = owner_ref[q : q + 1, :]
        row = row_ref[q : q + 1, :]
        hit = lax.broadcasted_iota(I32, (N_RE, K), 0) == owner
        one_hot = hit.astype(F32)
        earlier = jnp.dot(one_hot.astype(BF), before, preferred_element_type=F32)
        rank = jnp.sum(one_hot * earlier, axis=0, keepdims=True).astype(I32) + q * CAP
        slot_ref[q : q + 1, :] = owner * SLOTS + rank
        place = (lax.broadcasted_iota(I32, (LANES, K), 0) == rank).astype(F32).astype(BF)
        high = (one_hot * (row >> 4).astype(F32)).astype(BF)
        low = (one_hot * (row & 15).astype(F32)).astype(BF)
        contract = (((1,), (1,)), ((), ()))
        total += 16.0 * lax.dot_general(high, place, contract, preferred_element_type=F32)
        total += lax.dot_general(low, place, contract, preferred_element_type=F32)
    total = total.astype(I32)
    for o in range(N_RE):
        request_ref[o] = jnp.broadcast_to(total[o : o + 1, :], (8, LANES))


def mix_kernel(mode_ref, q_ref, rank_ref, rp_ref, table_ref, *out_refs):
    group = 8
    width = group * RP_LOCAL
    coords = rp_ref[...]
    lane_group = lax.broadcasted_iota(I32, (group, width), 1) // RP_LOCAL
    own = lane_group == lax.broadcasted_iota(I32, (group, width), 0)
    cosines, sines = [], []
    for q in range(Q):
        products = sum(q_ref[d, q] * coords[d : d + 1, :] for d in range(3)).astype(F32)
        cosine, sine = cos_sin(jnp.broadcast_to(products, (group, width)))
        cosines.append(jnp.where(own, cosine, 0.0))
        sines.append(jnp.where(own, sine, 0.0))
    left = jnp.concatenate(cosines + sines, axis=0).astype(BF)
    half = MODES * NB * NB
    low_lanes = lax.broadcasted_iota(I32, (group, LANES), 1) < LANES // 2
    rank = rank_ref[0]
    parts = [[[] for _ in range(Q * M_LOCAL)] for _ in range(N_RP)]
    for h in range(table_ref.shape[0] // group):
        values = table_ref[h * group : (h + 1) * group].reshape(width, 2 * half)
        sums = jnp.dot(left, values, preferred_element_type=F32)
        for q in range(Q):
            with_cos = sums[q * group : (q + 1) * group]
            with_sin = sums[(Q + q) * group : (Q + q + 1) * group]
            packed = []
            for p in range(MODES // 2):
                re_lanes = slice(p * LANES, (p + 1) * LANES)
                im_lanes = slice(half + p * LANES, half + (p + 1) * LANES)
                real = with_cos[:, re_lanes] - with_sin[:, im_lanes]
                imag = with_sin[:, re_lanes] + with_cos[:, im_lanes]
                packed.append(jnp.where(low_lanes, real, pltpu.roll(imag, LANES // 2, 1)))
                packed.append(jnp.where(low_lanes, pltpu.roll(real, LANES // 2, 1), imag))
            for s in range(N_RP):
                first = (rank ^ s) * M_LOCAL
                for n in range(M_LOCAL):
                    value = mode_ref[q, 0, first + n] * packed[0]
                    for mu in range(1, MODES):
                        value += mode_ref[q, mu, first + n] * packed[mu]
                    parts[s][q * M_LOCAL + n].append(value)
    for s in range(N_RP):
        for i in range(Q * M_LOCAL):
            out_refs[s][i] = jnp.concatenate(parts[s][i], axis=0).astype(BF)


def pack_kernel(own_ref, one_ref, two_ref, three_ref, request_ref, rotations_ref, out_ref):
    total = own_ref[...].astype(F32) + one_ref[...].astype(F32)
    total += two_ref[...].astype(F32) + three_ref[...].astype(F32)
    total = total.astype(BF)
    peers = out_ref.shape[0]
    wanted = request_ref[:, 0, :].T
    rows = lax.broadcasted_iota(I32, (SLOTS, K), 1)
    rotations = rotations_ref[...]
    for p in range(peers):
        out_ref[p, :ROWS, :] = total
        one_hot = (wanted[:SLOTS, p : p + 1] == rows).astype(F32).astype(BF)
        found = jnp.dot(one_hot, rotations, preferred_element_type=F32)
        out_ref[p, ROWS:, :] = found.astype(BF)


def phase_kernel(re_ref, k_ref, cos_ref, sin_ref):
    left = re_ref[...].astype(F32).astype(BF)
    right = k_ref[...].astype(F32).astype(BF)
    products = lax.dot_general(left, right, (((0,), (0,)), ((), ())), preferred_element_type=F32)
    cosine, sine = cos_sin(products)
    cos_ref[...] = cosine.astype(BF)
    sin_ref[...] = sine.astype(BF)


def final_kernel(slot_ref, rotations_ref, cos_ref, sin_ref, reply_ref, block_ref, out_ref, far_ref, near_ref, coupling_ref):
    step = pl.program_id(0)
    size = NB * NB

    @pl.when(step == 0)
    def _():
        near_ref[...] = rotations_ref[...].astype(F32).T
        replies = reply_ref[...].reshape(N_RE * SLOTS, LANES)
        for q in range(Q):
            slots = lax.broadcasted_iota(I32, (N_RE * SLOTS, K), 0)
            one_hot = (slots == slot_ref[q : q + 1, :]).astype(F32).astype(BF)
            far_ref[q] = lax.dot_general(replies, one_hot, (((0,), (0,)), ((), ())), preferred_element_type=F32)

    block = block_ref[...].reshape(RE, LANES)
    contract = (((0,), (0,)), ((), ()))
    with_cos = lax.dot_general(block, cos_ref[...], contract, preferred_element_type=F32)
    with_sin = lax.dot_general(block, sin_ref[...], contract, preferred_element_type=F32)
    coupling_ref[0:size] = with_cos[0:size] - with_sin[size:]
    coupling_ref[size:] = with_sin[0:size] + with_cos[size:]
    q = step // M_LOCAL
    for t in range(K // LANES):
        lanes = slice(t * LANES, (t + 1) * LANES)
        u_re = [near_ref[b * NB : (b + 1) * NB, lanes] for b in range(NB)]
        u_im = [near_ref[size + b * NB : size + (b + 1) * NB, lanes] for b in range(NB)]
        h_re, h_im = [], []
        for a in range(NB):
            acc_re = acc_im = None
            for b in range(NB):
                row = a * NB + b
                c_re = coupling_ref[row : row + 1, lanes]
                c_im = coupling_ref[size + row : size + row + 1, lanes]
                add_re = c_re * u_re[b] - c_im * u_im[b]
                add_im = c_re * u_im[b] + c_im * u_re[b]
                acc_re = add_re if acc_re is None else acc_re + add_re
                acc_im = add_im if acc_im is None else acc_im + add_im
            h_re.append(acc_re)
            h_im.append(acc_im)
        for pair in range(NB // 2):
            real, imag = [], []
            for m in (2 * pair, 2 * pair + 1):
                acc_re = acc_im = None
                for a in range(NB):
                    row = a * NB + m
                    v_re = far_ref[q, row : row + 1, lanes]
                    v_im = far_ref[q, size + row : size + row + 1, lanes]
                    add_re = v_re * h_re[a] + v_im * h_im[a]
                    add_im = v_re * h_im[a] - v_im * h_re[a]
                    acc_re = add_re if acc_re is None else acc_re + add_re
                    acc_im = add_im if acc_im is None else acc_im + add_im
                real.append(acc_re)
                imag.append(acc_im)
            rows = slice(pair * 16, pair * 16 + 16)
            out_ref[0, 0, rows, lanes] = jnp.concatenate(real, axis=0).astype(BF)
            out_ref[0, 1, rows, lanes] = jnp.concatenate(imag, axis=0).astype(BF)


def whole(shape):
    return pl.BlockSpec(shape, lambda *_: (0,) * len(shape))


def smem():
    return pl.BlockSpec(memory_space=pltpu.SMEM)


def params():
    return pltpu.CompilerParams(vmem_limit_bytes=48 << 20)


def local(
    wannier_table,
    mode_matrix,
    re_coords,
    rp_coords,
    q_coords,
    k_coords,
    rotations,
    kq_owner,
    kq_row,
):
    requests, slots = pl.pallas_call(
        requests_kernel,
        out_shape=(
            jax.ShapeDtypeStruct((N_RE, 8, LANES), I32),
            jax.ShapeDtypeStruct((Q, K), I32),
        ),
        compiler_params=params(),
        name="requests",
    )(kq_owner.reshape(Q, K), kq_row)
    wanted = lax.all_to_all(requests, "re", split_axis=0, concat_axis=0, tiled=True)

    chunk = 16
    block = (Q * M_LOCAL, chunk, LANES)
    parts = pl.pallas_call(
        mix_kernel,
        grid=(RE_LOCAL // chunk,),
        in_specs=[
            smem(),
            smem(),
            smem(),
            whole((3, 8 * RP_LOCAL)),
            pl.BlockSpec((chunk, RP_LOCAL, 2 * MODES * NB * NB), lambda i: (i, 0, 0)),
        ],
        out_specs=[pl.BlockSpec(block, lambda i: (0, i, 0))] * N_RP,
        out_shape=[jax.ShapeDtypeStruct((Q * M_LOCAL, RE_LOCAL, LANES), BF)] * N_RP,
        compiler_params=params(),
        name="mix",
    )(
        mode_matrix,
        q_coords,
        lax.axis_index("rp").reshape(1),
        jnp.tile(rp_coords, (1, 8)),
        wannier_table,
    )
    own = parts[0].reshape(ROWS, LANES)
    others = [
        lax.ppermute(parts[s].reshape(ROWS, LANES), "rp", [(j, j ^ s) for j in range(N_RP)])
        for s in range(1, N_RP)
    ]

    peers = 8
    packed = pl.pallas_call(
        pack_kernel,
        grid=(N_RE // peers,),
        in_specs=[whole((ROWS, LANES))] * N_RP
        + [pl.BlockSpec((peers, 8, LANES), lambda i: (i, 0, 0)), whole((K, LANES))],
        out_specs=pl.BlockSpec((peers, PACK, LANES), lambda i: (i, 0, 0)),
        out_shape=jax.ShapeDtypeStruct((N_RE, PACK, LANES), BF),
        compiler_params=params(),
        name="pack",
    )(own, *others, wanted, rotations)
    gathered = lax.all_to_all(packed, "re", split_axis=0, concat_axis=0, tiled=True)

    cosine, sine = pl.pallas_call(
        phase_kernel,
        grid=(4,),
        in_specs=[pl.BlockSpec((3, RE // 4), lambda i: (0, i)), whole((3, K))],
        out_specs=[pl.BlockSpec((RE // 4, K), lambda i: (i, 0))] * 2,
        out_shape=[jax.ShapeDtypeStruct((RE, K), BF)] * 2,
        compiler_params=params(),
        name="phase",
    )(re_coords, k_coords)

    result = pl.pallas_call(
        final_kernel,
        grid=(Q * M_LOCAL,),
        in_specs=[
            whole((Q, K)),
            whole((K, LANES)),
            whole((RE, K)),
            whole((RE, K)),
            pl.BlockSpec((N_RE, SLOTS, LANES), lambda i: (0, ROWS // SLOTS, 0)),
            pl.BlockSpec((N_RE, RE_LOCAL, LANES), lambda i: (0, i, 0)),
        ],
        out_specs=pl.BlockSpec((1, 2, NB * NB, K), lambda i: (i, 0, 0, 0)),
        out_shape=jax.ShapeDtypeStruct((Q * M_LOCAL, 2, NB * NB, K), BF),
        scratch_shapes=[
            pltpu.VMEM((Q, LANES, K), F32),
            pltpu.VMEM((LANES, K), F32),
            pltpu.VMEM((LANES, K), F32),
        ],
        compiler_params=params(),
        name="final",
    )(slots, rotations, cosine, sine, gathered, gathered)
    return result.reshape(Q, M_LOCAL, 2, NB * NB, K)


def solution(mesh):
    in_specs = (
        P("re", "rp", None),
        P(),
        P(),
        P(None, "rp"),
        P(),
        P(None, "re"),
        P("re", None),
        P(None, "re", None),
        P(None, "re"),
    )
    out_specs = P(None, "rp", None, None, "re")
    return jax.shard_map(local, mesh=mesh, in_specs=in_specs, out_specs=out_specs, check_vma=False)
```

```python
import math

import jax
import jax.numpy as jnp
from jax import lax
from jax.experimental import pallas as pl
from jax.experimental.pallas import tpu as pltpu
from jax.sharding import PartitionSpec as P

NB = 8
MODES = 12
Q = 2
GRID = 64
RE = 1024
RE_LOCAL = 32
RP_LOCAL = 32
K = 512
N_RE = 32
N_RP = 4
M_LOCAL = MODES // N_RP
CAP = 24
SLOTS = Q * CAP
ROWS = Q * M_LOCAL * RE_LOCAL
PACK = ROWS + SLOTS
LANES = 128
TURN = 2.0 * math.pi
SINE = [TURN ** n * s / math.factorial(n) for n, s in ((1, 1), (3, -1), (5, 1), (7, -1), (9, 1), (11, -1))]
BF = jnp.bfloat16
F32 = jnp.float32
I32 = jnp.int32


def sine_poly(t):
    s = t * t
    value = jnp.full_like(s, SINE[-1])
    for c in SINE[-2::-1]:
        value = value * s + c
    return value * t


def cos_sin(products):
    turns = products * (1.0 / GRID)
    frac = turns - jnp.floor(turns + 0.5)
    size = jnp.abs(frac)
    shifted = 0.25 - size
    cosine = sine_poly(shifted)
    folded = 0.25 - jnp.abs(shifted)
    sine = sine_poly(jnp.where(frac < 0.0, -folded, folded))
    return cosine, sine


def requests_kernel(owner_ref, row_ref, request_ref, slot_ref):
    before = (lax.broadcasted_iota(I32, (K, K), 0) < lax.broadcasted_iota(I32, (K, K), 1)).astype(F32).astype(BF)
    total = jnp.zeros((N_RE, LANES), F32)
    for q in range(Q):
        owner = owner_ref[q]
        row = row_ref[q : q + 1, :]
        hit = lax.broadcasted_iota(I32, (N_RE, K), 0) == owner
        one_hot = hit.astype(F32)
        earlier = jnp.dot(one_hot.astype(BF), before, preferred_element_type=F32)
        rank = jnp.sum(one_hot * earlier, axis=0, keepdims=True).astype(I32) + q * CAP
        slot_ref[q : q + 1, :] = owner * SLOTS + rank
        place = (lax.broadcasted_iota(I32, (LANES, K), 0) == rank).astype(F32).astype(BF)
        high = (one_hot * (row >> 4).astype(F32)).astype(BF)
        low = (one_hot * (row & 15).astype(F32)).astype(BF)
        contract = (((1,), (1,)), ((), ()))
        total += 16.0 * lax.dot_general(high, place, contract, preferred_element_type=F32)
        total += lax.dot_general(low, place, contract, preferred_element_type=F32)
    total = total.astype(I32)
    for o in range(N_RE):
        request_ref[o] = jnp.broadcast_to(total[o : o + 1, :], (8, LANES))


def mix_kernel(mode_ref, q_ref, rank_ref, rp_ref, table_ref, *out_refs):
    group = 8
    width = group * RP_LOCAL
    coords = jnp.concatenate([rp_ref[...]] * group, axis=1)
    lane_group = lax.broadcasted_iota(I32, (group, width), 1) // RP_LOCAL
    own = lane_group == lax.broadcasted_iota(I32, (group, width), 0)
    cosines, sines = [], []
    for q in range(Q):
        products = sum(q_ref[q, d] * coords[d : d + 1, :] for d in range(3)).astype(F32)
        cosine, sine = cos_sin(jnp.broadcast_to(products, (group, width)))
        cosines.append(jnp.where(own, cosine, 0.0))
        sines.append(jnp.where(own, sine, 0.0))
    left = jnp.concatenate(cosines + sines, axis=0).astype(BF)
    half = MODES * NB * NB
    low_lanes = lax.broadcasted_iota(I32, (group, LANES), 1) < LANES // 2
    rank = rank_ref[0]
    parts = [[[] for _ in range(Q * M_LOCAL)] for _ in range(N_RP)]
    for h in range(table_ref.shape[0] // group):
        values = table_ref[h * group : (h + 1) * group].reshape(width, 2 * half)
        sums = jnp.dot(left, values, preferred_element_type=F32)
        for q in range(Q):
            with_cos = sums[q * group : (q + 1) * group]
            with_sin = sums[(Q + q) * group : (Q + q + 1) * group]
            packed = []
            for p in range(MODES // 2):
                re_lanes = slice(p * LANES, (p + 1) * LANES)
                im_lanes = slice(half + p * LANES, half + (p + 1) * LANES)
                real = with_cos[:, re_lanes] - with_sin[:, im_lanes]
                imag = with_sin[:, re_lanes] + with_cos[:, im_lanes]
                packed.append(jnp.where(low_lanes, real, pltpu.roll(imag, LANES // 2, 1)))
                packed.append(jnp.where(low_lanes, pltpu.roll(real, LANES // 2, 1), imag))
            for s in range(N_RP):
                first = (rank ^ s) * M_LOCAL
                for n in range(M_LOCAL):
                    value = mode_ref[0, q, first + n] * packed[0]
                    for mu in range(1, MODES):
                        value += mode_ref[mu, q, first + n] * packed[mu]
                    parts[s][q * M_LOCAL + n].append(value)
    for s in range(N_RP):
        for i in range(Q * M_LOCAL):
            out_refs[s][i] = jnp.concatenate(parts[s][i], axis=0).astype(BF)


def pack_kernel(own_ref, one_ref, two_ref, three_ref, request_ref, rotations_ref, out_ref):
    total = own_ref[...].astype(F32) + one_ref[...].astype(F32)
    total += two_ref[...].astype(F32) + three_ref[...].astype(F32)
    total = total.astype(BF)
    peers = out_ref.shape[0]
    wanted = request_ref[:, 0, :].T
    rows = lax.broadcasted_iota(I32, (SLOTS, K), 1)
    rotations = rotations_ref[...]
    for p in range(peers):
        out_ref[p, :ROWS, :] = total
        one_hot = (wanted[:SLOTS, p : p + 1] == rows).astype(F32).astype(BF)
        found = jnp.dot(one_hot, rotations, preferred_element_type=F32)
        out_ref[p, ROWS:, :] = found.astype(BF)


def phase_kernel(re_ref, k_ref, out_ref):
    left = re_ref[...].astype(F32).astype(BF)
    right = k_ref[...].astype(F32).astype(BF)
    products = lax.dot_general(left, right, (((0,), (0,)), ((), ())), preferred_element_type=F32)
    cosine, sine = cos_sin(products)
    out_ref[0, :, :LANES] = cosine.astype(BF)
    out_ref[0, :, LANES:] = sine.astype(BF)


def final_kernel(slot_ref, rotations_ref, phase_ref, gathered_ref, out_ref, turned_ref, replies_ref, far_ref, near_ref, coupling_ref):
    size = NB * NB

    @pl.when(pl.program_id(0) == 0)
    def _():
        for i in range(Q * M_LOCAL):
            block = gathered_ref[:, i * RE_LOCAL : (i + 1) * RE_LOCAL, :].reshape(RE, LANES)
            turned_ref[i] = block.T
        replies_ref[...] = gathered_ref[:, ROWS:, :].reshape(N_RE * SLOTS, LANES).T

    near_ref[...] = rotations_ref[...].astype(F32).T
    slots = lax.broadcasted_iota(I32, (N_RE * SLOTS, LANES), 0)
    one_hot = [(slots == slot_ref[q : q + 1, :]).astype(F32).astype(BF) for q in range(Q)]
    far = jnp.dot(replies_ref[...], jnp.concatenate(one_hot, axis=1), preferred_element_type=F32)
    for q in range(Q):
        far_ref[q] = far[:, q * LANES : (q + 1) * LANES]
    u_re = [near_ref[b * NB : (b + 1) * NB] for b in range(NB)]
    u_im = [near_ref[size + b * NB : size + (b + 1) * NB] for b in range(NB)]
    for i in range(Q * M_LOCAL):
        q = i // M_LOCAL
        both = jnp.dot(turned_ref[i], phase_ref[0], preferred_element_type=F32)
        coupling_ref[i, :size] = both[:size, :LANES] - both[size:, LANES:]
        coupling_ref[i, size:] = both[:size, LANES:] + both[size:, :LANES]
        h_re, h_im = [], []
        for a in range(NB):
            acc_re = acc_im = None
            for b in range(NB):
                row = a * NB + b
                c_re = coupling_ref[i, row : row + 1]
                c_im = coupling_ref[i, size + row : size + row + 1]
                add_re = c_re * u_re[b] - c_im * u_im[b]
                add_im = c_re * u_im[b] + c_im * u_re[b]
                acc_re = add_re if acc_re is None else acc_re + add_re
                acc_im = add_im if acc_im is None else acc_im + add_im
            h_re.append(acc_re)
            h_im.append(acc_im)
        for pair in range(NB // 2):
            real, imag = [], []
            for m in (2 * pair, 2 * pair + 1):
                acc_re = acc_im = None
                for a in range(NB):
                    row = a * NB + m
                    v_re = far_ref[q, row : row + 1]
                    v_im = far_ref[q, size + row : size + row + 1]
                    add_re = v_re * h_re[a] + v_im * h_im[a]
                    add_im = v_re * h_im[a] - v_im * h_re[a]
                    acc_re = add_re if acc_re is None else acc_re + add_re
                    acc_im = add_im if acc_im is None else acc_im + add_im
                real.append(acc_re)
                imag.append(acc_im)
            rows = slice(pair * 16, pair * 16 + 16)
            out_ref[i, 0, rows] = jnp.concatenate(real, axis=0).astype(BF)
            out_ref[i, 1, rows] = jnp.concatenate(imag, axis=0).astype(BF)


def whole(shape):
    return pl.BlockSpec(shape, lambda *_: (0,) * len(shape))


def smem():
    return pl.BlockSpec(memory_space=pltpu.SMEM)


def in_hbm(array):
    return pltpu.with_memory_space_constraint(array, pltpu.HBM)


def params(mebibytes):
    return pltpu.CompilerParams(vmem_limit_bytes=mebibytes << 20)


def local(
    wannier_table,
    mode_matrix,
    re_coords,
    rp_coords,
    q_coords,
    k_coords,
    rotations,
    kq_owner,
    kq_row,
):
    chunk = 16
    block = (Q * M_LOCAL, chunk, LANES)
    parts = pl.pallas_call(
        mix_kernel,
        grid=(RE_LOCAL // chunk,),
        in_specs=[
            smem(),
            smem(),
            smem(),
            whole((3, RP_LOCAL)),
            pl.BlockSpec((chunk, RP_LOCAL, 2 * MODES * NB * NB), lambda i: (i, 0, 0)),
        ],
        out_specs=[pl.BlockSpec(block, lambda i: (0, i, 0))] * N_RP,
        out_shape=[jax.ShapeDtypeStruct((Q * M_LOCAL, RE_LOCAL, LANES), BF)] * N_RP,
        compiler_params=params(16),
        name="mix",
    )(
        in_hbm(mode_matrix.transpose(1, 0, 2)),
        in_hbm(q_coords.T),
        lax.axis_index("rp").reshape(1),
        in_hbm(rp_coords),
        in_hbm(wannier_table),
    )
    own = parts[0].reshape(ROWS, LANES)
    others = [
        lax.ppermute(parts[s].reshape(ROWS, LANES), "rp", [(j, j ^ s) for j in range(N_RP)])
        for s in range(1, N_RP)
    ]

    requests, slots = pl.pallas_call(
        requests_kernel,
        out_shape=(
            jax.ShapeDtypeStruct((N_RE, 8, LANES), I32),
            jax.ShapeDtypeStruct((Q, K), I32),
        ),
        compiler_params=params(16),
        name="requests",
    )(in_hbm(kq_owner.transpose(0, 2, 1)), in_hbm(kq_row))
    wanted = lax.all_to_all(requests, "re", split_axis=0, concat_axis=0, tiled=True)

    peers = 8
    packed = pl.pallas_call(
        pack_kernel,
        grid=(N_RE // peers,),
        in_specs=[whole((ROWS, LANES))] * N_RP
        + [pl.BlockSpec((peers, 8, LANES), lambda i: (i, 0, 0)), whole((K, LANES))],
        out_specs=pl.BlockSpec((peers, PACK, LANES), lambda i: (i, 0, 0)),
        out_shape=pltpu.HBM((N_RE, PACK, LANES), BF),
        compiler_params=params(16),
        name="pack",
    )(own, *others, wanted, rotations)
    gathered = lax.all_to_all(packed, "re", split_axis=0, concat_axis=0, tiled=True)

    tiles = K // LANES
    phases = pl.pallas_call(
        phase_kernel,
        grid=(tiles,),
        in_specs=[whole((3, RE)), pl.BlockSpec((3, LANES), lambda t: (0, t))],
        out_specs=pl.BlockSpec((1, RE, 2 * LANES), lambda t: (t, 0, 0)),
        out_shape=pltpu.HBM((tiles, RE, 2 * LANES), BF),
        compiler_params=params(16),
        name="phase",
    )(in_hbm(re_coords), in_hbm(k_coords))

    result = pl.pallas_call(
        final_kernel,
        grid=(tiles,),
        in_specs=[
            pl.BlockSpec((Q, LANES), lambda t: (0, t)),
            pl.BlockSpec((LANES, LANES), lambda t: (t, 0)),
            pl.BlockSpec((1, RE, 2 * LANES), lambda t: (t, 0, 0)),
            pl.BlockSpec(memory_space=pltpu.VMEM),
        ],
        out_specs=pl.BlockSpec((Q * M_LOCAL, 2, NB * NB, LANES), lambda t: (0, 0, 0, t)),
        out_shape=jax.ShapeDtypeStruct((Q * M_LOCAL, 2, NB * NB, K), BF),
        scratch_shapes=[
            pltpu.VMEM((Q * M_LOCAL, LANES, RE), BF),
            pltpu.VMEM((LANES, N_RE * SLOTS), BF),
            pltpu.VMEM((Q, LANES, LANES), F32),
            pltpu.VMEM((LANES, LANES), F32),
            pltpu.VMEM((Q * M_LOCAL, LANES, LANES), F32),
        ],
        compiler_params=params(16),
        name="final",
    )(slots, in_hbm(rotations), in_hbm(phases), gathered)
    return result.reshape(Q, M_LOCAL, 2, NB * NB, K)


def solution(mesh):
    in_specs = (
        P("re", "rp", None),
        P(),
        P(),
        P(None, "rp"),
        P(),
        P(None, "re"),
        P("re", None),
        P(None, "re", None),
        P(None, "re"),
    )
    out_specs = P(None, "rp", None, None, "re")
    return jax.shard_map(local, mesh=mesh, in_specs=in_specs, out_specs=out_specs, check_vma=False)
```

```python
import math

import jax
import jax.numpy as jnp
from jax import lax
from jax.experimental import pallas as pl
from jax.experimental.pallas import tpu as pltpu
from jax.sharding import PartitionSpec as P

NB = 8
MODES = 12
Q = 2
GRID = 64
RE = 1024
RE_LOCAL = 32
RP_LOCAL = 32
K = 512
N_RE = 32
N_RP = 4
M_LOCAL = MODES // N_RP
CAP = 24
SLOTS = Q * CAP
ROWS = Q * M_LOCAL * RE_LOCAL
PACK = ROWS + SLOTS
LANES = 128
TURN = 2.0 * math.pi
SINE = [TURN ** n * s / math.factorial(n) for n, s in ((1, 1), (3, -1), (5, 1), (7, -1), (9, 1), (11, -1))]
BF = jnp.bfloat16
F32 = jnp.float32
I32 = jnp.int32


def sine_poly(t):
    s = t * t
    value = jnp.full_like(s, SINE[-1])
    for c in SINE[-2::-1]:
        value = value * s + c
    return value * t


def cos_sin(products):
    turns = products * (1.0 / GRID)
    frac = turns - jnp.floor(turns + 0.5)
    size = jnp.abs(frac)
    shifted = 0.25 - size
    cosine = sine_poly(shifted)
    folded = 0.25 - jnp.abs(shifted)
    sine = sine_poly(jnp.where(frac < 0.0, -folded, folded))
    return cosine, sine


def requests_kernel(owner_ref, row_ref, request_ref, slot_ref):
    before = (lax.broadcasted_iota(I32, (K, K), 0) < lax.broadcasted_iota(I32, (K, K), 1)).astype(F32).astype(BF)
    total = jnp.zeros((N_RE, LANES), F32)
    for q in range(Q):
        owner = owner_ref[q]
        row = row_ref[q : q + 1, :]
        hit = lax.broadcasted_iota(I32, (N_RE, K), 0) == owner
        one_hot = hit.astype(F32)
        earlier = jnp.dot(one_hot.astype(BF), before, preferred_element_type=F32)
        rank = jnp.sum(one_hot * earlier, axis=0, keepdims=True).astype(I32) + q * CAP
        slot_ref[q : q + 1, :] = owner * SLOTS + rank
        place = (lax.broadcasted_iota(I32, (LANES, K), 0) == rank).astype(F32).astype(BF)
        high = (one_hot * (row >> 4).astype(F32)).astype(BF)
        low = (one_hot * (row & 15).astype(F32)).astype(BF)
        contract = (((1,), (1,)), ((), ()))
        total += 16.0 * lax.dot_general(high, place, contract, preferred_element_type=F32)
        total += lax.dot_general(low, place, contract, preferred_element_type=F32)
    total = total.astype(I32)
    for o in range(N_RE):
        request_ref[o] = total[o : o + 1, :]


def mix_kernel(mode_ref, q_ref, rank_ref, rp_ref, table_ref, *out_refs):
    group = 8
    width = group * RP_LOCAL
    coords = jnp.concatenate([rp_ref[...]] * group, axis=1)
    lane_group = lax.broadcasted_iota(I32, (group, width), 1) // RP_LOCAL
    own = lane_group == lax.broadcasted_iota(I32, (group, width), 0)
    cosines, sines = [], []
    for q in range(Q):
        products = sum(q_ref[q, d] * coords[d : d + 1, :] for d in range(3)).astype(F32)
        cosine, sine = cos_sin(jnp.broadcast_to(products, (group, width)))
        cosines.append(jnp.where(own, cosine, 0.0))
        sines.append(jnp.where(own, sine, 0.0))
    left = jnp.concatenate(cosines + sines, axis=0).astype(BF)
    half = MODES * NB * NB
    low_lanes = lax.broadcasted_iota(I32, (group, LANES), 1) < LANES // 2
    rank = rank_ref[0]
    parts = [[[] for _ in range(Q * M_LOCAL)] for _ in range(N_RP)]
    for h in range(table_ref.shape[0] // group):
        values = table_ref[h * group : (h + 1) * group].reshape(width, 2 * half)
        sums = jnp.dot(left, values, preferred_element_type=F32)
        for q in range(Q):
            with_cos = sums[q * group : (q + 1) * group]
            with_sin = sums[(Q + q) * group : (Q + q + 1) * group]
            packed = []
            for p in range(MODES // 2):
                re_lanes = slice(p * LANES, (p + 1) * LANES)
                im_lanes = slice(half + p * LANES, half + (p + 1) * LANES)
                real = with_cos[:, re_lanes] - with_sin[:, im_lanes]
                imag = with_sin[:, re_lanes] + with_cos[:, im_lanes]
                packed.append(jnp.where(low_lanes, real, pltpu.roll(imag, LANES // 2, 1)))
                packed.append(jnp.where(low_lanes, pltpu.roll(real, LANES // 2, 1), imag))
            for s in range(N_RP):
                first = (rank ^ s) * M_LOCAL
                for n in range(M_LOCAL):
                    value = mode_ref[0, q, first + n] * packed[0]
                    for mu in range(1, MODES):
                        value += mode_ref[mu, q, first + n] * packed[mu]
                    parts[s][q * M_LOCAL + n].append(value)
    for s in range(N_RP):
        for i in range(Q * M_LOCAL):
            out_refs[s][i] = jnp.concatenate(parts[s][i], axis=0).astype(BF)


def pack_kernel(own_ref, one_ref, two_ref, three_ref, request_ref, rotations_ref, out_ref):
    total = own_ref[...].astype(F32) + one_ref[...].astype(F32)
    total += two_ref[...].astype(F32) + three_ref[...].astype(F32)
    total = total.astype(BF)
    peers = out_ref.shape[0]
    wanted = request_ref[:, 0, :].T
    rows = lax.broadcasted_iota(I32, (SLOTS, K), 1)
    rotations = rotations_ref[...]
    for p in range(peers):
        out_ref[p, :ROWS, :] = total
        one_hot = (wanted[:SLOTS, p : p + 1] == rows).astype(F32).astype(BF)
        found = jnp.dot(one_hot, rotations, preferred_element_type=F32)
        out_ref[p, ROWS:, :] = found.astype(BF)


def phase_kernel(re_ref, k_ref, out_ref):
    left = re_ref[...].astype(F32).astype(BF)
    right = k_ref[...].astype(F32).astype(BF)
    products = lax.dot_general(left, right, (((0,), (0,)), ((), ())), preferred_element_type=F32)
    cosine, sine = cos_sin(products)
    out_ref[0, :, :LANES] = cosine.astype(BF)
    out_ref[0, :, LANES:] = sine.astype(BF)


def final_kernel(slot_ref, rotations_ref, phase_ref, gathered_ref, out_ref, turned_ref, replies_ref, far_ref, near_ref, coupling_ref):
    size = NB * NB

    @pl.when(pl.program_id(0) == 0)
    def _():
        for i in range(Q * M_LOCAL):
            block = gathered_ref[:, i * RE_LOCAL : (i + 1) * RE_LOCAL, :].reshape(RE, LANES)
            turned_ref[i] = block.T
        replies_ref[...] = gathered_ref[:, ROWS:, :].reshape(N_RE * SLOTS, LANES).T

    near_ref[...] = rotations_ref[...].astype(F32).T
    slots = lax.broadcasted_iota(I32, (N_RE * SLOTS, LANES), 0)
    one_hot = [(slots == slot_ref[q : q + 1, :]).astype(F32).astype(BF) for q in range(Q)]
    far = jnp.dot(replies_ref[...], jnp.concatenate(one_hot, axis=1), preferred_element_type=F32)
    for q in range(Q):
        far_ref[q] = far[:, q * LANES : (q + 1) * LANES]
    u_re = [near_ref[b * NB : (b + 1) * NB] for b in range(NB)]
    u_im = [near_ref[size + b * NB : size + (b + 1) * NB] for b in range(NB)]
    for i in range(Q * M_LOCAL):
        q = i // M_LOCAL
        both = jnp.dot(turned_ref[i], phase_ref[0], preferred_element_type=F32)
        coupling_ref[i, :size] = both[:size, :LANES] - both[size:, LANES:]
        coupling_ref[i, size:] = both[:size, LANES:] + both[size:, :LANES]
        h_re, h_im = [], []
        for a in range(NB):
            acc_re = acc_im = None
            for b in range(NB):
                row = a * NB + b
                c_re = coupling_ref[i, row : row + 1]
                c_im = coupling_ref[i, size + row : size + row + 1]
                add_re = c_re * u_re[b] - c_im * u_im[b]
                add_im = c_re * u_im[b] + c_im * u_re[b]
                acc_re = add_re if acc_re is None else acc_re + add_re
                acc_im = add_im if acc_im is None else acc_im + add_im
            h_re.append(acc_re)
            h_im.append(acc_im)
        for pair in range(NB // 2):
            real, imag = [], []
            for m in (2 * pair, 2 * pair + 1):
                acc_re = acc_im = None
                for a in range(NB):
                    row = a * NB + m
                    v_re = far_ref[q, row : row + 1]
                    v_im = far_ref[q, size + row : size + row + 1]
                    add_re = v_re * h_re[a] + v_im * h_im[a]
                    add_im = v_re * h_im[a] - v_im * h_re[a]
                    acc_re = add_re if acc_re is None else acc_re + add_re
                    acc_im = add_im if acc_im is None else acc_im + add_im
                real.append(acc_re)
                imag.append(acc_im)
            rows = slice(pair * 16, pair * 16 + 16)
            out_ref[i, 0, rows] = jnp.concatenate(real, axis=0).astype(BF)
            out_ref[i, 1, rows] = jnp.concatenate(imag, axis=0).astype(BF)


def whole(shape):
    return pl.BlockSpec(shape, lambda *_: (0,) * len(shape))


def smem():
    return pl.BlockSpec(memory_space=pltpu.SMEM)


def in_hbm(array):
    return pltpu.with_memory_space_constraint(array, pltpu.HBM)


def params(mebibytes):
    return pltpu.CompilerParams(vmem_limit_bytes=mebibytes << 20)


def local(
    wannier_table,
    mode_matrix,
    re_coords,
    rp_coords,
    q_coords,
    k_coords,
    rotations,
    kq_owner,
    kq_row,
):
    chunk = 16
    block = (Q * M_LOCAL, chunk, LANES)
    parts = pl.pallas_call(
        mix_kernel,
        grid=(RE_LOCAL // chunk,),
        in_specs=[
            smem(),
            smem(),
            smem(),
            whole((3, RP_LOCAL)),
            pl.BlockSpec((chunk, RP_LOCAL, 2 * MODES * NB * NB), lambda i: (i, 0, 0)),
        ],
        out_specs=[pl.BlockSpec(block, lambda i: (0, i, 0))] * N_RP,
        out_shape=[jax.ShapeDtypeStruct((Q * M_LOCAL, RE_LOCAL, LANES), BF)] * N_RP,
        compiler_params=params(16),
        name="mix",
    )(
        in_hbm(mode_matrix.transpose(1, 0, 2)),
        in_hbm(q_coords.T),
        lax.axis_index("rp").reshape(1),
        in_hbm(rp_coords),
        in_hbm(wannier_table),
    )
    own = parts[0].reshape(ROWS, LANES)
    others = [
        lax.ppermute(parts[s].reshape(ROWS, LANES), "rp", [(j, j ^ s) for j in range(N_RP)])
        for s in range(1, N_RP)
    ]

    requests, slots = pl.pallas_call(
        requests_kernel,
        out_shape=(
            jax.ShapeDtypeStruct((N_RE, 1, LANES), I32),
            jax.ShapeDtypeStruct((Q, K), I32),
        ),
        compiler_params=params(16),
        name="requests",
    )(in_hbm(kq_owner.transpose(0, 2, 1)), in_hbm(kq_row))
    wanted = lax.all_to_all(requests, "re", split_axis=0, concat_axis=0, tiled=True)

    peers = 8
    packed = pl.pallas_call(
        pack_kernel,
        grid=(N_RE // peers,),
        in_specs=[whole((ROWS, LANES))] * N_RP
        + [pl.BlockSpec((peers, 1, LANES), lambda i: (i, 0, 0)), whole((K, LANES))],
        out_specs=pl.BlockSpec((peers, PACK, LANES), lambda i: (i, 0, 0)),
        out_shape=pltpu.HBM((N_RE, PACK, LANES), BF),
        compiler_params=params(16),
        name="pack",
    )(own, *others, wanted, rotations)
    gathered = lax.all_to_all(packed, "re", split_axis=0, concat_axis=0, tiled=True)

    tiles = K // LANES
    phases = pl.pallas_call(
        phase_kernel,
        grid=(tiles,),
        in_specs=[whole((3, RE)), pl.BlockSpec((3, LANES), lambda t: (0, t))],
        out_specs=pl.BlockSpec((1, RE, 2 * LANES), lambda t: (t, 0, 0)),
        out_shape=pltpu.HBM((tiles, RE, 2 * LANES), BF),
        compiler_params=params(16),
        name="phase",
    )(in_hbm(re_coords), in_hbm(k_coords))

    result = pl.pallas_call(
        final_kernel,
        grid=(tiles,),
        in_specs=[
            pl.BlockSpec((Q, LANES), lambda t: (0, t)),
            pl.BlockSpec((LANES, LANES), lambda t: (t, 0)),
            pl.BlockSpec((1, RE, 2 * LANES), lambda t: (t, 0, 0)),
            pl.BlockSpec(memory_space=pltpu.VMEM),
        ],
        out_specs=pl.BlockSpec((Q * M_LOCAL, 2, NB * NB, LANES), lambda t: (0, 0, 0, t)),
        out_shape=jax.ShapeDtypeStruct((Q * M_LOCAL, 2, NB * NB, K), BF),
        scratch_shapes=[
            pltpu.VMEM((Q * M_LOCAL, LANES, RE), BF),
            pltpu.VMEM((LANES, N_RE * SLOTS), BF),
            pltpu.VMEM((Q, LANES, LANES), F32),
            pltpu.VMEM((LANES, LANES), F32),
            pltpu.VMEM((Q * M_LOCAL, LANES, LANES), F32),
        ],
        compiler_params=params(16),
        name="final",
    )(slots, in_hbm(rotations), in_hbm(phases), gathered)
    return result.reshape(Q, M_LOCAL, 2, NB * NB, K)


def solution(mesh):
    in_specs = (
        P("re", "rp", None),
        P(),
        P(),
        P(None, "rp"),
        P(),
        P(None, "re"),
        P("re", None),
        P(None, "re", None),
        P(None, "re"),
    )
    out_specs = P(None, "rp", None, None, "re")
    return jax.shard_map(local, mesh=mesh, in_specs=in_specs, out_specs=out_specs, check_vma=False)
```

```python
import math

import jax
import jax.numpy as jnp
from jax import lax
from jax.experimental import pallas as pl
from jax.experimental.pallas import tpu as pltpu
from jax.sharding import PartitionSpec as P

NB = 8
MODES = 12
Q = 2
GRID = 64
RE = 1024
RE_LOCAL = 32
RP_LOCAL = 32
K = 512
N_RE = 32
N_RP = 4
M_LOCAL = MODES // N_RP
CAP = 24
SLOTS = Q * CAP
ROWS = Q * M_LOCAL * RE_LOCAL
PACK = ROWS + SLOTS
LANES = 128
TILES = K // LANES
SIZE = NB * NB
TURN = 2.0 * math.pi
SINE = [TURN ** n * s / math.factorial(n) for n, s in ((1, 1), (3, -1), (5, 1), (7, -1), (9, 1), (11, -1))]
BF = jnp.bfloat16
F32 = jnp.float32
I32 = jnp.int32


def sine_poly(t):
    s = t * t
    value = jnp.full_like(s, SINE[-1])
    for c in SINE[-2::-1]:
        value = value * s + c
    return value * t


def cos_sin(products):
    turns = products * (1.0 / GRID)
    frac = turns - jnp.floor(turns + 0.5)
    size = jnp.abs(frac)
    shifted = 0.25 - size
    cosine = sine_poly(shifted)
    folded = 0.25 - jnp.abs(shifted)
    sine = sine_poly(jnp.where(frac < 0.0, -folded, folded))
    return cosine, sine


def requests_kernel(owner_ref, row_ref, request_ref, slot_ref):
    before = (lax.broadcasted_iota(I32, (K, K), 0) < lax.broadcasted_iota(I32, (K, K), 1)).astype(F32).astype(BF)
    total = jnp.zeros((N_RE, LANES), F32)
    for q in range(Q):
        owner = owner_ref[q]
        row = row_ref[q : q + 1, :]
        hit = lax.broadcasted_iota(I32, (N_RE, K), 0) == owner
        one_hot = hit.astype(F32)
        earlier = jnp.dot(one_hot.astype(BF), before, preferred_element_type=F32)
        rank = jnp.sum(one_hot * earlier, axis=0, keepdims=True).astype(I32) + q * CAP
        slot_ref[q : q + 1, :] = owner * CAP + rank - q * CAP
        place = (lax.broadcasted_iota(I32, (LANES, K), 0) == rank).astype(F32).astype(BF)
        high = (one_hot * (row >> 4).astype(F32)).astype(BF)
        low = (one_hot * (row & 15).astype(F32)).astype(BF)
        contract = (((1,), (1,)), ((), ()))
        total += 16.0 * lax.dot_general(high, place, contract, preferred_element_type=F32)
        total += lax.dot_general(low, place, contract, preferred_element_type=F32)
    total = total.astype(I32)
    for o in range(N_RE):
        request_ref[o] = total[o : o + 1, :]


def mix_kernel(mode_ref, q_ref, rank_ref, rp_ref, table_ref, *out_refs):
    group = 8
    width = group * RP_LOCAL
    coords = jnp.concatenate([rp_ref[...]] * group, axis=1)
    lane_group = lax.broadcasted_iota(I32, (group, width), 1) // RP_LOCAL
    own = lane_group == lax.broadcasted_iota(I32, (group, width), 0)
    cosines, sines = [], []
    for q in range(Q):
        products = sum(q_ref[q, d] * coords[d : d + 1, :] for d in range(3)).astype(F32)
        cosine, sine = cos_sin(jnp.broadcast_to(products, (group, width)))
        cosines.append(jnp.where(own, cosine, 0.0))
        sines.append(jnp.where(own, sine, 0.0))
    left = jnp.concatenate(cosines + sines, axis=0).astype(BF)
    half = MODES * NB * NB
    low_lanes = lax.broadcasted_iota(I32, (group, LANES), 1) < LANES // 2
    rank = rank_ref[0]
    parts = [[[] for _ in range(Q * M_LOCAL)] for _ in range(N_RP)]
    for h in range(table_ref.shape[0] // group):
        values = table_ref[h * group : (h + 1) * group].reshape(width, 2 * half)
        sums = jnp.dot(left, values, preferred_element_type=F32)
        for q in range(Q):
            with_cos = sums[q * group : (q + 1) * group]
            with_sin = sums[(Q + q) * group : (Q + q + 1) * group]
            packed = []
            for p in range(MODES // 2):
                re_lanes = slice(p * LANES, (p + 1) * LANES)
                im_lanes = slice(half + p * LANES, half + (p + 1) * LANES)
                real = with_cos[:, re_lanes] - with_sin[:, im_lanes]
                imag = with_sin[:, re_lanes] + with_cos[:, im_lanes]
                packed.append(jnp.where(low_lanes, real, pltpu.roll(imag, LANES // 2, 1)))
                packed.append(jnp.where(low_lanes, pltpu.roll(real, LANES // 2, 1), imag))
            for s in range(N_RP):
                first = (rank ^ s) * M_LOCAL
                for n in range(M_LOCAL):
                    value = mode_ref[0, q, first + n] * packed[0]
                    for mu in range(1, MODES):
                        value += mode_ref[mu, q, first + n] * packed[mu]
                    parts[s][q * M_LOCAL + n].append(value)
    for s in range(N_RP):
        for i in range(Q * M_LOCAL):
            out_refs[s][i] = jnp.concatenate(parts[s][i], axis=0).astype(BF)


def sum_kernel(own_ref, one_ref, two_ref, three_ref, out_ref):
    total = own_ref[...].astype(F32) + one_ref[...].astype(F32)
    total += two_ref[...].astype(F32) + three_ref[...].astype(F32)
    out_ref[...] = jnp.broadcast_to(total.astype(BF)[None], out_ref.shape)


def lookup_kernel(packed_ref, request_ref, rotations_ref, out_ref):
    peers = out_ref.shape[0]
    wanted = request_ref[:, 0, :].T
    rows = lax.broadcasted_iota(I32, (SLOTS, K), 1)
    one_hot = [(wanted[:SLOTS, p : p + 1] == rows).astype(F32).astype(BF) for p in range(peers)]
    found = jnp.dot(jnp.concatenate(one_hot, axis=0), rotations_ref[...], preferred_element_type=F32)
    out_ref[...] = found.reshape(peers, SLOTS, LANES).astype(BF)


def phase_kernel(re_ref, k_ref, slot_ref, rotations_ref, out_ref, pick_ref, near_ref):
    left = re_ref[...].astype(F32).astype(BF)
    right = k_ref[...].astype(F32).astype(BF)
    products = lax.dot_general(left, right, (((0,), (0,)), ((), ())), preferred_element_type=F32)
    cosine, sine = cos_sin(products)
    out_ref[0, :, :LANES] = cosine.astype(BF)
    out_ref[0, :, LANES:] = sine.astype(BF)
    place = lax.broadcasted_iota(I32, (N_RE * CAP, LANES), 0)
    for q in range(Q):
        pick_ref[q] = (place == slot_ref[q : q + 1, :]).astype(F32).astype(BF)
    near = rotations_ref[...].astype(F32).T
    near_ref[: 2 * SIZE] = near
    near_ref[2 * SIZE :] = near[:SIZE] + near[SIZE:]


def chain(terms):
    total = None
    for term in terms:
        total = term if total is None else total + term
    return total


def rotate(coupling_ref, far_ref, near_ref, out_ref, q, i, t):
    lanes = slice(t * LANES, (t + 1) * LANES)
    near = [[near_ref[o * SIZE + b * NB : o * SIZE + (b + 1) * NB, lanes] for b in range(NB)] for o in range(3)]
    halves = []
    for a in range(NB):
        real, imag, both = [
            chain(coupling_ref[o * SIZE + a * NB + b : o * SIZE + a * NB + b + 1] * near[o][b] for b in range(NB))
            for o in range(3)
        ]
        half = real - imag, both - (real + imag)
        halves.append((*half, half[0] + half[1]))
    for pair in range(NB // 2):
        results = [], []
        for m in (2 * pair, 2 * pair + 1):
            real, imag, both = [
                chain(far_ref[q, o * SIZE + a * NB + m : o * SIZE + a * NB + m + 1, lanes] * halves[a][o] for a in range(NB))
                for o in range(3)
            ]
            results[0].append(real + imag)
            results[1].append(both - (real - imag))
        rows = slice(pair * 2 * NB, (pair + 1) * 2 * NB)
        for c in range(2):
            out_ref[t, i, c, rows] = jnp.concatenate(results[c], axis=0).astype(BF)


def final_kernel(
    phase_hbm, pick_hbm, near_hbm, gathered_ref, out_hbm,
    phase_ref, pick_ref, near_ref, turned_ref, far_ref, coupling_ref, out_ref, phase_sem, pick_sem, near_sem, out_sem,
):
    phase_copies = [pltpu.make_async_copy(phase_hbm.at[t], phase_ref.at[t], phase_sem.at[t]) for t in range(TILES)]
    pick_copy = pltpu.make_async_copy(pick_hbm, pick_ref, pick_sem)
    near_copy = pltpu.make_async_copy(near_hbm, near_ref, near_sem)
    out_copies = [
        pltpu.make_async_copy(out_ref.at[t], out_hbm.at[:, :, :, t * LANES : (t + 1) * LANES], out_sem.at[t])
        for t in range(TILES)
    ]
    pick_copy.start()
    phase_copies[0].start()
    near_copy.start()
    for t in range(1, TILES):
        phase_copies[t].start()
    replies = gathered_ref[:, ROWS:, :].astype(F32)
    turned = []
    for q in range(Q):
        rows = replies[:, q * CAP : (q + 1) * CAP, :].reshape(N_RE * CAP, LANES)
        turned.append(rows.T.astype(BF))
    for i in range(Q * M_LOCAL):
        block = gathered_ref[:, i * RE_LOCAL : (i + 1) * RE_LOCAL, :].reshape(RE, LANES)
        turned_ref[i] = block.T
    pick_copy.wait()
    for q in range(Q):
        far = jnp.dot(turned[q], pick_ref[q], preferred_element_type=F32)
        far_ref[q, : 2 * SIZE] = far
        far_ref[q, 2 * SIZE :] = far[:SIZE] - far[SIZE:]

    def couple(t, i):
        both = jnp.dot(turned_ref[i], phase_ref[t], preferred_element_type=F32)
        real = both[:SIZE, :LANES] - both[SIZE:, LANES:]
        imag = both[:SIZE, LANES:] + both[SIZE:, :LANES]
        coupling_ref[t % 2, i, :SIZE] = real
        coupling_ref[t % 2, i, SIZE : 2 * SIZE] = imag
        coupling_ref[t % 2, i, 2 * SIZE :] = real + imag

    phase_copies[0].wait()
    for i in range(Q * M_LOCAL):
        couple(0, i)
    near_copy.wait()
    for t in range(TILES):
        if t + 1 < TILES:
            phase_copies[t + 1].wait()
        for i in range(Q * M_LOCAL):
            if t + 1 < TILES:
                couple(t + 1, i)
            rotate(coupling_ref.at[t % 2, i], far_ref, near_ref, out_ref, i // M_LOCAL, i, t)
        out_copies[t].start()
    for t in range(TILES):
        out_copies[t].wait()


def whole(shape):
    return pl.BlockSpec(shape, lambda *_: (0,) * len(shape))


def smem():
    return pl.BlockSpec(memory_space=pltpu.SMEM)


def in_hbm(array):
    return pltpu.with_memory_space_constraint(array, pltpu.HBM)


def params(mebibytes):
    return pltpu.CompilerParams(vmem_limit_bytes=mebibytes << 20)


def local(
    wannier_table,
    mode_matrix,
    re_coords,
    rp_coords,
    q_coords,
    k_coords,
    rotations,
    kq_owner,
    kq_row,
):
    chunk = 16
    block = (Q * M_LOCAL, chunk, LANES)
    parts = pl.pallas_call(
        mix_kernel,
        grid=(RE_LOCAL // chunk,),
        in_specs=[
            smem(),
            smem(),
            smem(),
            whole((3, RP_LOCAL)),
            pl.BlockSpec((chunk, RP_LOCAL, 2 * MODES * NB * NB), lambda i: (i, 0, 0)),
        ],
        out_specs=[pl.BlockSpec(block, lambda i: (0, i, 0))] * N_RP,
        out_shape=[jax.ShapeDtypeStruct((Q * M_LOCAL, RE_LOCAL, LANES), BF)] * N_RP,
        compiler_params=params(16),
        name="mix",
    )(
        in_hbm(mode_matrix.transpose(1, 0, 2)),
        in_hbm(q_coords.T),
        lax.axis_index("rp").reshape(1),
        in_hbm(rp_coords),
        in_hbm(wannier_table),
    )
    own = parts[0].reshape(ROWS, LANES)
    others = [
        lax.ppermute(parts[s].reshape(ROWS, LANES), "rp", [(j, j ^ s) for j in range(N_RP)])
        for s in range(1, N_RP)
    ]

    requests, slots = pl.pallas_call(
        requests_kernel,
        out_shape=(
            jax.ShapeDtypeStruct((N_RE, 1, LANES), I32),
            jax.ShapeDtypeStruct((Q, K), I32),
        ),
        compiler_params=params(16),
        name="requests",
    )(in_hbm(kq_owner.transpose(0, 2, 1)), in_hbm(kq_row))
    wanted = lax.all_to_all(requests, "re", split_axis=0, concat_axis=0, tiled=True)

    peers = 8
    spread = pl.pallas_call(
        sum_kernel,
        grid=(N_RE // peers,),
        in_specs=[whole((ROWS, LANES))] * N_RP,
        out_specs=pl.BlockSpec((peers, ROWS, LANES), lambda i: (i, 0, 0)),
        out_shape=pltpu.HBM((N_RE, PACK, LANES), BF),
        compiler_params=params(8),
        name="sum",
    )(own, *others)
    packed = pl.pallas_call(
        lookup_kernel,
        grid=(N_RE // peers,),
        in_specs=[
            pl.BlockSpec(memory_space=pltpu.HBM),
            pl.BlockSpec((peers, 1, LANES), lambda i: (i, 0, 0)),
            whole((K, LANES)),
        ],
        out_specs=pl.BlockSpec((peers, SLOTS, LANES), lambda i: (i, ROWS // SLOTS, 0)),
        out_shape=pltpu.HBM((N_RE, PACK, LANES), BF),
        input_output_aliases={0: 0},
        compiler_params=params(8),
        name="lookup",
    )(spread, wanted, rotations)
    gathered = lax.all_to_all(packed, "re", split_axis=0, concat_axis=0, tiled=True)

    phases, picks, near = pl.pallas_call(
        phase_kernel,
        grid=(TILES,),
        in_specs=[
            whole((3, RE)),
            pl.BlockSpec((3, LANES), lambda t: (0, t)),
            pl.BlockSpec((Q, LANES), lambda t: (0, t)),
            pl.BlockSpec((LANES, LANES), lambda t: (t, 0)),
        ],
        out_specs=[
            pl.BlockSpec((1, RE, 2 * LANES), lambda t: (t, 0, 0)),
            pl.BlockSpec((Q, N_RE * CAP, LANES), lambda t: (0, 0, t)),
            pl.BlockSpec((3 * SIZE, LANES), lambda t: (0, t)),
        ],
        out_shape=[
            pltpu.HBM((TILES, RE, 2 * LANES), BF),
            pltpu.HBM((Q, N_RE * CAP, K), BF),
            pltpu.HBM((3 * SIZE, K), F32),
        ],
        compiler_params=params(16),
        name="phase",
    )(in_hbm(re_coords), in_hbm(k_coords), slots, in_hbm(rotations))

    hbm = pl.BlockSpec(memory_space=pltpu.HBM)
    result = pl.pallas_call(
        final_kernel,
        in_specs=[hbm, hbm, hbm, pl.BlockSpec(memory_space=pltpu.VMEM)],
        out_specs=hbm,
        out_shape=jax.ShapeDtypeStruct((Q * M_LOCAL, 2, SIZE, K), BF),
        scratch_shapes=[
            pltpu.VMEM((TILES, RE, 2 * LANES), BF),
            pltpu.VMEM((Q, N_RE * CAP, K), BF),
            pltpu.VMEM((3 * SIZE, K), F32),
            pltpu.VMEM((Q * M_LOCAL, LANES, RE), BF),
            pltpu.VMEM((Q, 3 * SIZE, K), F32),
            pltpu.VMEM((2, Q * M_LOCAL, 3 * SIZE, LANES), F32),
            pltpu.VMEM((TILES, Q * M_LOCAL, 2, SIZE, LANES), BF),
            pltpu.SemaphoreType.DMA((TILES,)),
            pltpu.SemaphoreType.DMA,
            pltpu.SemaphoreType.DMA,
            pltpu.SemaphoreType.DMA((TILES,)),
        ],
        compiler_params=params(24),
        name="final",
    )(in_hbm(phases), in_hbm(picks), in_hbm(near), gathered)
    return result.reshape(Q, M_LOCAL, 2, NB * NB, K)


def solution(mesh):
    in_specs = (
        P("re", "rp", None),
        P(),
        P(),
        P(None, "rp"),
        P(),
        P(None, "re"),
        P("re", None),
        P(None, "re", None),
        P(None, "re"),
    )
    out_specs = P(None, "rp", None, None, "re")
    return jax.shard_map(local, mesh=mesh, in_specs=in_specs, out_specs=out_specs, check_vma=False)
```

```python
import math

import jax
import jax.numpy as jnp
from jax import lax
from jax.experimental import pallas as pl
from jax.experimental.pallas import tpu as pltpu
from jax.sharding import PartitionSpec as P

NB = 8
MODES = 12
Q = 2
GRID = 64
RE = 1024
RE_LOCAL = 32
RP_LOCAL = 32
K = 512
N_RE = 32
N_RP = 4
M_LOCAL = MODES // N_RP
CAP = 24
SLOTS = Q * CAP
ROWS = Q * M_LOCAL * RE_LOCAL
PACK = ROWS + SLOTS
LANES = 128
TILES = K // LANES
FIRST = 2
SIZE = NB * NB
TURN = 2.0 * math.pi
SINE = [TURN ** n * s / math.factorial(n) for n, s in ((1, 1), (3, -1), (5, 1), (7, -1), (9, 1), (11, -1))]
BF = jnp.bfloat16
F32 = jnp.float32
I32 = jnp.int32


def sine_poly(t):
    s = t * t
    value = jnp.full_like(s, SINE[-1])
    for c in SINE[-2::-1]:
        value = value * s + c
    return value * t


def cos_sin(products):
    turns = products * (1.0 / GRID)
    frac = turns - jnp.floor(turns + 0.5)
    size = jnp.abs(frac)
    shifted = 0.25 - size
    cosine = sine_poly(shifted)
    folded = 0.25 - jnp.abs(shifted)
    sine = sine_poly(jnp.where(frac < 0.0, -folded, folded))
    return cosine, sine


def requests_kernel(owner_ref, row_ref, request_ref, slot_ref):
    before = (lax.broadcasted_iota(I32, (K, K), 0) < lax.broadcasted_iota(I32, (K, K), 1)).astype(F32).astype(BF)
    total = jnp.zeros((N_RE, LANES), F32)
    for q in range(Q):
        owner = owner_ref[q]
        row = row_ref[q : q + 1, :]
        hit = lax.broadcasted_iota(I32, (N_RE, K), 0) == owner
        one_hot = hit.astype(F32)
        earlier = jnp.dot(one_hot.astype(BF), before, preferred_element_type=F32)
        rank = jnp.sum(one_hot * earlier, axis=0, keepdims=True).astype(I32) + q * CAP
        slot_ref[q : q + 1, :] = owner * CAP + rank - q * CAP
        place = (lax.broadcasted_iota(I32, (LANES, K), 0) == rank).astype(F32).astype(BF)
        high = (one_hot * (row >> 4).astype(F32)).astype(BF)
        low = (one_hot * (row & 15).astype(F32)).astype(BF)
        contract = (((1,), (1,)), ((), ()))
        total += 16.0 * lax.dot_general(high, place, contract, preferred_element_type=F32)
        total += lax.dot_general(low, place, contract, preferred_element_type=F32)
    total = total.astype(I32)
    for o in range(N_RE):
        request_ref[o] = total[o : o + 1, :]


def mix_kernel(mode_ref, q_ref, rank_ref, rp_ref, table_ref, *out_refs):
    group = 8
    width = group * RP_LOCAL
    coords = jnp.concatenate([rp_ref[...]] * group, axis=1)
    lane_group = lax.broadcasted_iota(I32, (group, width), 1) // RP_LOCAL
    own = lane_group == lax.broadcasted_iota(I32, (group, width), 0)
    cosines, sines = [], []
    for q in range(Q):
        products = sum(q_ref[q, d] * coords[d : d + 1, :] for d in range(3)).astype(F32)
        cosine, sine = cos_sin(jnp.broadcast_to(products, (group, width)))
        cosines.append(jnp.where(own, cosine, 0.0))
        sines.append(jnp.where(own, sine, 0.0))
    left = jnp.concatenate(cosines + sines, axis=0).astype(BF)
    half = MODES * NB * NB
    low_lanes = lax.broadcasted_iota(I32, (group, LANES), 1) < LANES // 2
    rank = rank_ref[0]
    parts = [[[] for _ in range(Q * M_LOCAL)] for _ in range(N_RP)]
    for h in range(table_ref.shape[0] // group):
        values = table_ref[h * group : (h + 1) * group].reshape(width, 2 * half)
        sums = jnp.dot(left, values, preferred_element_type=F32)
        for q in range(Q):
            with_cos = sums[q * group : (q + 1) * group]
            with_sin = sums[(Q + q) * group : (Q + q + 1) * group]
            packed = []
            for p in range(MODES // 2):
                re_lanes = slice(p * LANES, (p + 1) * LANES)
                im_lanes = slice(half + p * LANES, half + (p + 1) * LANES)
                real = with_cos[:, re_lanes] - with_sin[:, im_lanes]
                imag = with_sin[:, re_lanes] + with_cos[:, im_lanes]
                packed.append(jnp.where(low_lanes, real, pltpu.roll(imag, LANES // 2, 1)))
                packed.append(jnp.where(low_lanes, pltpu.roll(real, LANES // 2, 1), imag))
            for s in range(N_RP):
                first = (rank ^ s) * M_LOCAL
                for n in range(M_LOCAL):
                    value = mode_ref[0, q, first + n] * packed[0]
                    for mu in range(1, MODES):
                        value += mode_ref[mu, q, first + n] * packed[mu]
                    parts[s][q * M_LOCAL + n].append(value)
    for s in range(N_RP):
        for i in range(Q * M_LOCAL):
            out_refs[s][i] = jnp.concatenate(parts[s][i], axis=0).astype(BF)


def sum_kernel(own_ref, one_ref, two_ref, three_ref, out_ref):
    total = own_ref[...].astype(F32) + one_ref[...].astype(F32)
    total += two_ref[...].astype(F32) + three_ref[...].astype(F32)
    out_ref[...] = jnp.broadcast_to(total.astype(BF)[None], out_ref.shape)


def lookup_kernel(packed_ref, request_ref, rotations_ref, out_ref):
    peers = out_ref.shape[0]
    wanted = request_ref[:, 0, :].T
    rows = lax.broadcasted_iota(I32, (SLOTS, K), 1)
    one_hot = [(wanted[:SLOTS, p : p + 1] == rows).astype(F32).astype(BF) for p in range(peers)]
    found = jnp.dot(jnp.concatenate(one_hot, axis=0), rotations_ref[...], preferred_element_type=F32)
    out_ref[...] = found.reshape(peers, SLOTS, LANES).astype(BF)


def phase_kernel(re_ref, k_ref, out_ref):
    left = re_ref[...].astype(F32).astype(BF)
    for t in range(out_ref.shape[0]):
        right = k_ref[:, t * LANES : (t + 1) * LANES].astype(F32).astype(BF)
        products = lax.dot_general(left, right, (((0,), (0,)), ((), ())), preferred_element_type=F32)
        cosine, sine = cos_sin(products)
        out_ref[t, :, :LANES] = cosine.astype(BF)
        out_ref[t, :, LANES:] = sine.astype(BF)


def chain(terms):
    total = None
    for term in terms:
        total = term if total is None else total + term
    return total


def rotate(coupling_ref, far_ref, near_ref, out_ref, q, i, t):
    lanes = slice(t * LANES, (t + 1) * LANES)
    near = [[near_ref[o * SIZE + b * NB : o * SIZE + (b + 1) * NB, lanes] for b in range(NB)] for o in range(3)]
    halves = []
    for a in range(NB):
        real, imag, both = [
            chain(coupling_ref[o * SIZE + a * NB + b : o * SIZE + a * NB + b + 1] * near[o][b] for b in range(NB))
            for o in range(3)
        ]
        half = real - imag, both - (real + imag)
        halves.append((*half, half[0] + half[1]))
    for pair in range(NB // 2):
        results = [], []
        for m in (2 * pair, 2 * pair + 1):
            real, imag, both = [
                chain(far_ref[q, o * SIZE + a * NB + m : o * SIZE + a * NB + m + 1, lanes] * halves[a][o] for a in range(NB))
                for o in range(3)
            ]
            results[0].append(real + imag)
            results[1].append(both - (real - imag))
        rows = slice(pair * 2 * NB, (pair + 1) * 2 * NB)
        for c in range(2):
            out_ref[t, i, c, rows] = jnp.concatenate(results[c], axis=0).astype(BF)


def final_kernel(
    slot_ref, rotations_ref, first_ref, later_hbm, gathered_ref, out_hbm,
    later_ref, near_ref, turned_ref, far_ref, coupling_ref, out_ref, later_sem, out_sem,
):
    later = [pltpu.make_async_copy(later_hbm.at[t], later_ref.at[t], later_sem.at[t]) for t in range(TILES - FIRST)]
    out_copies = [
        pltpu.make_async_copy(out_ref.at[t], out_hbm.at[:, :, :, t * LANES : (t + 1) * LANES], out_sem.at[t])
        for t in range(TILES)
    ]
    for copy in later:
        copy.start()
    near = rotations_ref[...].astype(F32).T
    near_ref[: 2 * SIZE] = near
    near_ref[2 * SIZE :] = near[:SIZE] + near[SIZE:]
    replies = gathered_ref[:, ROWS:, :].astype(F32)
    place = lax.broadcasted_iota(I32, (N_RE * CAP, K), 0)
    for q in range(Q):
        rows = replies[:, q * CAP : (q + 1) * CAP, :].reshape(N_RE * CAP, LANES)
        one_hot = (place == slot_ref[q : q + 1, :]).astype(F32).astype(BF)
        far = jnp.dot(rows.T.astype(BF), one_hot, preferred_element_type=F32)
        far_ref[q, : 2 * SIZE] = far
        far_ref[q, 2 * SIZE :] = far[:SIZE] - far[SIZE:]
    for i in range(Q * M_LOCAL):
        block = gathered_ref[:, i * RE_LOCAL : (i + 1) * RE_LOCAL, :].reshape(RE, LANES)
        turned_ref[i] = block.T

    def couple(t, i):
        phase = first_ref[t] if t < FIRST else later_ref[t - FIRST]
        both = jnp.dot(turned_ref[i], phase, preferred_element_type=F32)
        real = both[:SIZE, :LANES] - both[SIZE:, LANES:]
        imag = both[:SIZE, LANES:] + both[SIZE:, :LANES]
        coupling_ref[t % 2, i, :SIZE] = real
        coupling_ref[t % 2, i, SIZE : 2 * SIZE] = imag
        coupling_ref[t % 2, i, 2 * SIZE :] = real + imag

    for i in range(Q * M_LOCAL):
        couple(0, i)
    for t in range(TILES):
        if FIRST <= t + 1 < TILES:
            later[t + 1 - FIRST].wait()
        for i in range(Q * M_LOCAL):
            if t + 1 < TILES:
                couple(t + 1, i)
            rotate(coupling_ref.at[t % 2, i], far_ref, near_ref, out_ref, i // M_LOCAL, i, t)
        out_copies[t].start()
    for t in range(TILES):
        out_copies[t].wait()


def whole(shape):
    return pl.BlockSpec(shape, lambda *_: (0,) * len(shape))


def smem():
    return pl.BlockSpec(memory_space=pltpu.SMEM)


def in_hbm(array):
    return pltpu.with_memory_space_constraint(array, pltpu.HBM)


def params(mebibytes):
    return pltpu.CompilerParams(vmem_limit_bytes=mebibytes << 20)


def local(
    wannier_table,
    mode_matrix,
    re_coords,
    rp_coords,
    q_coords,
    k_coords,
    rotations,
    kq_owner,
    kq_row,
):
    chunk = 16
    block = (Q * M_LOCAL, chunk, LANES)
    parts = pl.pallas_call(
        mix_kernel,
        grid=(RE_LOCAL // chunk,),
        in_specs=[
            smem(),
            smem(),
            smem(),
            whole((3, RP_LOCAL)),
            pl.BlockSpec((chunk, RP_LOCAL, 2 * MODES * NB * NB), lambda i: (i, 0, 0)),
        ],
        out_specs=[pl.BlockSpec(block, lambda i: (0, i, 0))] * N_RP,
        out_shape=[jax.ShapeDtypeStruct((Q * M_LOCAL, RE_LOCAL, LANES), BF)] * N_RP,
        compiler_params=params(16),
        name="mix",
    )(
        in_hbm(mode_matrix.transpose(1, 0, 2)),
        in_hbm(q_coords.T),
        lax.axis_index("rp").reshape(1),
        in_hbm(rp_coords),
        in_hbm(wannier_table),
    )
    own = parts[0].reshape(ROWS, LANES)
    others = [
        lax.ppermute(parts[s].reshape(ROWS, LANES), "rp", [(j, j ^ s) for j in range(N_RP)])
        for s in range(1, N_RP)
    ]

    requests, slots = pl.pallas_call(
        requests_kernel,
        out_shape=(
            jax.ShapeDtypeStruct((N_RE, 1, LANES), I32),
            jax.ShapeDtypeStruct((Q, K), I32),
        ),
        compiler_params=params(16),
        name="requests",
    )(in_hbm(kq_owner.transpose(0, 2, 1)), in_hbm(kq_row))
    wanted = lax.all_to_all(requests, "re", split_axis=0, concat_axis=0, tiled=True)

    peers = 8
    spread = pl.pallas_call(
        sum_kernel,
        grid=(N_RE // peers,),
        in_specs=[whole((ROWS, LANES))] * N_RP,
        out_specs=pl.BlockSpec((peers, ROWS, LANES), lambda i: (i, 0, 0)),
        out_shape=pltpu.HBM((N_RE, PACK, LANES), BF),
        compiler_params=params(8),
        name="sum",
    )(own, *others)
    packed = pl.pallas_call(
        lookup_kernel,
        grid=(1,),
        in_specs=[
            pl.BlockSpec(memory_space=pltpu.HBM),
            pl.BlockSpec(memory_space=pltpu.VMEM),
            pl.BlockSpec(memory_space=pltpu.VMEM),
        ],
        out_specs=pl.BlockSpec((N_RE, SLOTS, LANES), lambda i: (0, ROWS // SLOTS, 0)),
        out_shape=pltpu.HBM((N_RE, PACK, LANES), BF),
        input_output_aliases={0: 0},
        compiler_params=params(8),
        name="lookup",
    )(spread, wanted, rotations)
    gathered = lax.all_to_all(packed, "re", split_axis=0, concat_axis=0, tiled=True)

    def phase_tiles(coords, space):
        tiles = coords.shape[1] // LANES
        return pl.pallas_call(
            phase_kernel,
            out_shape=space((tiles, RE, 2 * LANES), BF),
            compiler_params=params(16),
            name="phase",
        )(in_hbm(re_coords), in_hbm(coords))

    first = phase_tiles(k_coords[:, : FIRST * LANES], pltpu.VMEM)
    later = phase_tiles(k_coords[:, FIRST * LANES :], pltpu.HBM)

    hbm = pl.BlockSpec(memory_space=pltpu.HBM)
    vmem = pl.BlockSpec(memory_space=pltpu.VMEM)
    result = pl.pallas_call(
        final_kernel,
        in_specs=[vmem, vmem, vmem, hbm, vmem],
        out_specs=hbm,
        out_shape=jax.ShapeDtypeStruct((Q * M_LOCAL, 2, SIZE, K), BF),
        scratch_shapes=[
            pltpu.VMEM((TILES - FIRST, RE, 2 * LANES), BF),
            pltpu.VMEM((3 * SIZE, K), F32),
            pltpu.VMEM((Q * M_LOCAL, LANES, RE), BF),
            pltpu.VMEM((Q, 3 * SIZE, K), F32),
            pltpu.VMEM((2, Q * M_LOCAL, 3 * SIZE, LANES), F32),
            pltpu.VMEM((TILES, Q * M_LOCAL, 2, SIZE, LANES), BF),
            pltpu.SemaphoreType.DMA((TILES - FIRST,)),
            pltpu.SemaphoreType.DMA((TILES,)),
        ],
        compiler_params=params(24),
        name="final",
    )(slots, rotations, first, in_hbm(later), gathered)
    return result.reshape(Q, M_LOCAL, 2, NB * NB, K)


def solution(mesh):
    in_specs = (
        P("re", "rp", None),
        P(),
        P(),
        P(None, "rp"),
        P(),
        P(None, "re"),
        P("re", None),
        P(None, "re", None),
        P(None, "re"),
    )
    out_specs = P(None, "rp", None, None, "re")
    return jax.shard_map(local, mesh=mesh, in_specs=in_specs, out_specs=out_specs, check_vma=False)
```

```python
import math

import jax
import jax.numpy as jnp
from jax import lax
from jax.experimental import pallas as pl
from jax.experimental.pallas import tpu as pltpu
from jax.sharding import PartitionSpec as P

NB = 8
MODES = 12
Q = 2
GRID = 64
RE = 1024
RE_LOCAL = 32
RP_LOCAL = 32
K = 512
N_RE = 32
N_RP = 4
M_LOCAL = MODES // N_RP
CAP = 24
SLOTS = Q * CAP
ROWS = Q * M_LOCAL * RE_LOCAL
PACK = ROWS + SLOTS
LANES = 128
TILES = K // LANES
FIRST = 2
PIECES = 8
SIZE = NB * NB
TURN = 2.0 * math.pi
SINE = [TURN ** n * s / math.factorial(n) for n, s in ((1, 1), (3, -1), (5, 1), (7, -1), (9, 1), (11, -1))]
BF = jnp.bfloat16
F32 = jnp.float32
I32 = jnp.int32


def sine_poly(t):
    s = t * t
    value = jnp.full_like(s, SINE[-1])
    for c in SINE[-2::-1]:
        value = value * s + c
    return value * t


def cos_sin(products):
    turns = products * (1.0 / GRID)
    frac = turns - jnp.floor(turns + 0.5)
    size = jnp.abs(frac)
    shifted = 0.25 - size
    cosine = sine_poly(shifted)
    folded = 0.25 - jnp.abs(shifted)
    sine = sine_poly(jnp.where(frac < 0.0, -folded, folded))
    return cosine, sine


def find_requests(owner_ref, row_ref, request_ref, slot_ref):
    before = (lax.broadcasted_iota(I32, (K, K), 0) < lax.broadcasted_iota(I32, (K, K), 1)).astype(F32).astype(BF)
    total = jnp.zeros((N_RE, LANES), F32)
    for q in range(Q):
        owner = owner_ref[q]
        row = row_ref[q : q + 1, :]
        hit = lax.broadcasted_iota(I32, (N_RE, K), 0) == owner
        one_hot = hit.astype(F32)
        earlier = jnp.dot(one_hot.astype(BF), before, preferred_element_type=F32)
        rank = jnp.sum(one_hot * earlier, axis=0, keepdims=True).astype(I32)
        slot_ref[q : q + 1, :] = owner * CAP + rank
        place = (lax.broadcasted_iota(I32, (LANES, K), 0) == rank + q * CAP).astype(F32).astype(BF)
        high = (one_hot * (row >> 4).astype(F32)).astype(BF)
        low = (one_hot * (row & 15).astype(F32)).astype(BF)
        contract = (((1,), (1,)), ((), ()))
        total += 16.0 * lax.dot_general(high, place, contract, preferred_element_type=F32)
        total += lax.dot_general(low, place, contract, preferred_element_type=F32)
    total = total.astype(I32)
    for o in range(N_RE):
        request_ref[o] = total[o : o + 1, :]


def mix_kernel(
    mode_ref, q_ref, rank_ref, rp_ref, owner_ref, row_ref, table_hbm,
    own_ref, one_ref, two_ref, three_ref, request_ref, slot_ref, table_ref, sem,
):
    out_refs = own_ref, one_ref, two_ref, three_ref
    piece = RE_LOCAL // PIECES
    copies = [
        pltpu.make_async_copy(
            table_hbm.at[c * piece : (c + 1) * piece], table_ref.at[c * piece : (c + 1) * piece], sem.at[c]
        )
        for c in range(PIECES)
    ]
    for copy in copies:
        copy.start()
    find_requests(owner_ref, row_ref, request_ref, slot_ref)
    group = 8
    width = group * RP_LOCAL
    coords = jnp.concatenate([rp_ref[...]] * group, axis=1)
    lane_group = lax.broadcasted_iota(I32, (group, width), 1) // RP_LOCAL
    own = lane_group == lax.broadcasted_iota(I32, (group, width), 0)
    cosines, sines = [], []
    for q in range(Q):
        products = sum(q_ref[q, d] * coords[d : d + 1, :] for d in range(3)).astype(F32)
        cosine, sine = cos_sin(jnp.broadcast_to(products, (group, width)))
        cosines.append(jnp.where(own, cosine, 0.0))
        sines.append(jnp.where(own, sine, 0.0))
    left = jnp.concatenate(cosines + sines, axis=0).astype(BF)
    half = MODES * NB * NB
    low_lanes = lax.broadcasted_iota(I32, (group, LANES), 1) < LANES // 2
    rank = rank_ref[0]
    for pair in range(RE_LOCAL // (2 * group)):
        parts = [[[] for _ in range(Q * M_LOCAL)] for _ in range(N_RP)]
        for h in (2 * pair, 2 * pair + 1):
            for copy in copies[h * group // piece : (h + 1) * group // piece]:
                copy.wait()
            values = table_ref[h * group : (h + 1) * group].reshape(width, 2 * half)
            sums = jnp.dot(left, values, preferred_element_type=F32)
            for q in range(Q):
                with_cos = sums[q * group : (q + 1) * group]
                with_sin = sums[(Q + q) * group : (Q + q + 1) * group]
                packed = []
                for p in range(MODES // 2):
                    re_lanes = slice(p * LANES, (p + 1) * LANES)
                    im_lanes = slice(half + p * LANES, half + (p + 1) * LANES)
                    real = with_cos[:, re_lanes] - with_sin[:, im_lanes]
                    imag = with_sin[:, re_lanes] + with_cos[:, im_lanes]
                    packed.append(jnp.where(low_lanes, real, pltpu.roll(imag, LANES // 2, 1)))
                    packed.append(jnp.where(low_lanes, pltpu.roll(real, LANES // 2, 1), imag))
                for s in range(N_RP):
                    first = (rank ^ s) * M_LOCAL
                    for n in range(M_LOCAL):
                        value = mode_ref[0, q, first + n] * packed[0]
                        for mu in range(1, MODES):
                            value += mode_ref[mu, q, first + n] * packed[mu]
                        parts[s][q * M_LOCAL + n].append(value)
        rows = slice(pair * 2 * group, (pair + 1) * 2 * group)
        for s in range(N_RP):
            for i in range(Q * M_LOCAL):
                out_refs[s][i, rows] = jnp.concatenate(parts[s][i], axis=0).astype(BF)


def sum_kernel(own_ref, one_ref, two_ref, three_ref, out_hbm, total_ref, sem):
    total = own_ref[...].astype(F32) + one_ref[...].astype(F32)
    total += two_ref[...].astype(F32) + three_ref[...].astype(F32)
    total_ref[...] = total.astype(BF)
    copies = [pltpu.make_async_copy(total_ref, out_hbm.at[p, :ROWS, :], sem.at[p]) for p in range(N_RE)]
    for copy in copies:
        copy.start()
    for copy in copies:
        copy.wait()


def lookup_kernel(packed_ref, request_ref, rotations_ref, out_ref):
    peers = out_ref.shape[0]
    wanted = request_ref[:, 0, :].T
    rows = lax.broadcasted_iota(I32, (SLOTS, K), 1)
    one_hot = [(wanted[:SLOTS, p : p + 1] == rows).astype(F32).astype(BF) for p in range(peers)]
    found = jnp.dot(jnp.concatenate(one_hot, axis=0), rotations_ref[...], preferred_element_type=F32)
    out_ref[...] = found.reshape(peers, SLOTS, LANES).astype(BF)


def phase_kernel(re_ref, k_ref, out_ref):
    left = re_ref[...].astype(F32).astype(BF)
    for t in range(out_ref.shape[0]):
        right = k_ref[:, t * LANES : (t + 1) * LANES].astype(F32).astype(BF)
        products = lax.dot_general(left, right, (((0,), (0,)), ((), ())), preferred_element_type=F32)
        cosine, sine = cos_sin(products)
        out_ref[t, :, :LANES] = cosine.astype(BF)
        out_ref[t, :, LANES:] = sine.astype(BF)


def chain(terms):
    total = None
    for term in terms:
        total = term if total is None else total + term
    return total


def rotate(coupling_ref, far_ref, near_ref, out_ref, q, i, t):
    lanes = slice(t * LANES, (t + 1) * LANES)
    near = [[near_ref[o * SIZE + b * NB : o * SIZE + (b + 1) * NB, lanes] for b in range(NB)] for o in range(3)]
    halves = []
    for a in range(NB):
        real, imag, both = [
            chain(coupling_ref[o * SIZE + a * NB + b : o * SIZE + a * NB + b + 1] * near[o][b] for b in range(NB))
            for o in range(3)
        ]
        half = real - imag, both - (real + imag)
        halves.append((*half, half[0] + half[1]))
    for pair in range(NB // 2):
        results = [], []
        for m in (2 * pair, 2 * pair + 1):
            real, imag, both = [
                chain(far_ref[q, o * SIZE + a * NB + m : o * SIZE + a * NB + m + 1, lanes] * halves[a][o] for a in range(NB))
                for o in range(3)
            ]
            results[0].append(real + imag)
            results[1].append(both - (real - imag))
        rows = slice(pair * 2 * NB, (pair + 1) * 2 * NB)
        for c in range(2):
            out_ref[t, i, c, rows] = jnp.concatenate(results[c], axis=0).astype(BF)


def final_kernel(
    slot_ref, rotations_ref, first_ref, later_hbm, gathered_ref, out_hbm,
    later_ref, near_ref, turned_ref, far_ref, coupling_ref, out_ref, later_sem, out_sem,
):
    later = [pltpu.make_async_copy(later_hbm.at[t], later_ref.at[t], later_sem.at[t]) for t in range(TILES - FIRST)]
    out_copies = [
        pltpu.make_async_copy(out_ref.at[t], out_hbm.at[:, :, :, t * LANES : (t + 1) * LANES], out_sem.at[t])
        for t in range(TILES)
    ]
    for copy in later:
        copy.start()
    near = rotations_ref[...].astype(F32).T
    near_ref[: 2 * SIZE] = near
    near_ref[2 * SIZE :] = near[:SIZE] + near[SIZE:]
    replies = gathered_ref[:, ROWS:, :].astype(F32)
    place = lax.broadcasted_iota(I32, (N_RE * CAP, K), 0)
    for q in range(Q):
        rows = replies[:, q * CAP : (q + 1) * CAP, :].reshape(N_RE * CAP, LANES)
        one_hot = (place == slot_ref[q : q + 1, :]).astype(F32).astype(BF)
        far = jnp.dot(rows.T.astype(BF), one_hot, preferred_element_type=F32)
        far_ref[q, : 2 * SIZE] = far
        far_ref[q, 2 * SIZE :] = far[:SIZE] - far[SIZE:]
    for i in range(Q * M_LOCAL):
        block = gathered_ref[:, i * RE_LOCAL : (i + 1) * RE_LOCAL, :].reshape(RE, LANES)
        turned_ref[i] = block.T

    def couple(t, i):
        phase = first_ref[t] if t < FIRST else later_ref[t - FIRST]
        both = jnp.dot(turned_ref[i], phase, preferred_element_type=F32)
        real = both[:SIZE, :LANES] - both[SIZE:, LANES:]
        imag = both[:SIZE, LANES:] + both[SIZE:, :LANES]
        coupling_ref[t % 2, i, :SIZE] = real
        coupling_ref[t % 2, i, SIZE : 2 * SIZE] = imag
        coupling_ref[t % 2, i, 2 * SIZE :] = real + imag

    for i in range(Q * M_LOCAL):
        couple(0, i)
    for t in range(TILES):
        if FIRST <= t + 1 < TILES:
            later[t + 1 - FIRST].wait()
        for i in range(Q * M_LOCAL):
            if t + 1 < TILES:
                couple(t + 1, i)
            rotate(coupling_ref.at[t % 2, i], far_ref, near_ref, out_ref, i // M_LOCAL, i, t)
        out_copies[t].start()
    for t in range(TILES):
        out_copies[t].wait()


def whole(shape):
    return pl.BlockSpec(shape, lambda *_: (0,) * len(shape))


def smem():
    return pl.BlockSpec(memory_space=pltpu.SMEM)


def in_hbm(array):
    return pltpu.with_memory_space_constraint(array, pltpu.HBM)


def params(mebibytes):
    return pltpu.CompilerParams(vmem_limit_bytes=mebibytes << 20)


def local(
    wannier_table,
    mode_matrix,
    re_coords,
    rp_coords,
    q_coords,
    k_coords,
    rotations,
    kq_owner,
    kq_row,
):
    hbm = pl.BlockSpec(memory_space=pltpu.HBM)
    vmem = pl.BlockSpec(memory_space=pltpu.VMEM)
    *parts, requests, slots = pl.pallas_call(
        mix_kernel,
        in_specs=[smem(), smem(), smem(), vmem, vmem, vmem, hbm],
        out_shape=[jax.ShapeDtypeStruct((Q * M_LOCAL, RE_LOCAL, LANES), BF)] * N_RP
        + [jax.ShapeDtypeStruct((N_RE, 1, LANES), I32), jax.ShapeDtypeStruct((Q, K), I32)],
        scratch_shapes=[
            pltpu.VMEM((RE_LOCAL, RP_LOCAL, 2 * MODES * SIZE), BF),
            pltpu.SemaphoreType.DMA((PIECES,)),
        ],
        compiler_params=params(16),
        name="mix",
    )(
        in_hbm(mode_matrix.transpose(1, 0, 2)),
        in_hbm(q_coords.T),
        lax.axis_index("rp").reshape(1),
        in_hbm(rp_coords),
        in_hbm(kq_owner.transpose(0, 2, 1)),
        in_hbm(kq_row),
        in_hbm(wannier_table),
    )
    own = parts[0].reshape(ROWS, LANES)
    others = [
        lax.ppermute(parts[s].reshape(ROWS, LANES), "rp", [(j, j ^ s) for j in range(N_RP)])
        for s in range(1, N_RP)
    ]

    wanted = lax.all_to_all(requests, "re", split_axis=0, concat_axis=0, tiled=True)

    spread = pl.pallas_call(
        sum_kernel,
        in_specs=[vmem] * N_RP,
        out_specs=hbm,
        out_shape=pltpu.HBM((N_RE, PACK, LANES), BF),
        scratch_shapes=[pltpu.VMEM((ROWS, LANES), BF), pltpu.SemaphoreType.DMA((N_RE,))],
        compiler_params=params(8),
        name="sum",
    )(own, *others)
    packed = pl.pallas_call(
        lookup_kernel,
        grid=(1,),
        in_specs=[
            pl.BlockSpec(memory_space=pltpu.HBM),
            pl.BlockSpec(memory_space=pltpu.VMEM),
            pl.BlockSpec(memory_space=pltpu.VMEM),
        ],
        out_specs=pl.BlockSpec((N_RE, SLOTS, LANES), lambda i: (0, ROWS // SLOTS, 0)),
        out_shape=pltpu.HBM((N_RE, PACK, LANES), BF),
        input_output_aliases={0: 0},
        compiler_params=params(8),
        name="lookup",
    )(spread, wanted, rotations)
    gathered = lax.all_to_all(packed, "re", split_axis=0, concat_axis=0, tiled=True)

    def phase_tiles(coords, space):
        tiles = coords.shape[1] // LANES
        return pl.pallas_call(
            phase_kernel,
            out_shape=space((tiles, RE, 2 * LANES), BF),
            compiler_params=params(16),
            name="phase",
        )(in_hbm(re_coords), in_hbm(coords))

    first = phase_tiles(k_coords[:, : FIRST * LANES], pltpu.VMEM)
    later = phase_tiles(k_coords[:, FIRST * LANES :], pltpu.HBM)

    result = pl.pallas_call(
        final_kernel,
        in_specs=[vmem, vmem, vmem, hbm, vmem],
        out_specs=hbm,
        out_shape=jax.ShapeDtypeStruct((Q * M_LOCAL, 2, SIZE, K), BF),
        scratch_shapes=[
            pltpu.VMEM((TILES - FIRST, RE, 2 * LANES), BF),
            pltpu.VMEM((3 * SIZE, K), F32),
            pltpu.VMEM((Q * M_LOCAL, LANES, RE), BF),
            pltpu.VMEM((Q, 3 * SIZE, K), F32),
            pltpu.VMEM((2, Q * M_LOCAL, 3 * SIZE, LANES), F32),
            pltpu.VMEM((TILES, Q * M_LOCAL, 2, SIZE, LANES), BF),
            pltpu.SemaphoreType.DMA((TILES - FIRST,)),
            pltpu.SemaphoreType.DMA((TILES,)),
        ],
        compiler_params=params(24),
        name="final",
    )(slots, rotations, first, in_hbm(later), gathered)
    return result.reshape(Q, M_LOCAL, 2, NB * NB, K)


def solution(mesh):
    in_specs = (
        P("re", "rp", None),
        P(),
        P(),
        P(None, "rp"),
        P(),
        P(None, "re"),
        P("re", None),
        P(None, "re", None),
        P(None, "re"),
    )
    out_specs = P(None, "rp", None, None, "re")
    return jax.shard_map(local, mesh=mesh, in_specs=in_specs, out_specs=out_specs, check_vma=False)
```

```python
import math

import jax
import jax.numpy as jnp
from jax import lax
from jax.experimental import pallas as pl
from jax.experimental.pallas import tpu as pltpu
from jax.sharding import PartitionSpec as P

NB = 8
MODES = 12
Q = 2
GRID = 64
RE = 1024
RE_LOCAL = 32
RP_LOCAL = 32
K = 512
N_RE = 32
N_RP = 4
M_LOCAL = MODES // N_RP
CAP = 24
SLOTS = Q * CAP
ROWS = Q * M_LOCAL * RE_LOCAL
PACK = ROWS + SLOTS
LANES = 128
TILES = K // LANES
FIRST = 2
CHUNK = 16
SIZE = NB * NB
TURN = 2.0 * math.pi
SINE = [TURN ** n * s / math.factorial(n) for n, s in ((1, 1), (3, -1), (5, 1), (7, -1), (9, 1), (11, -1))]
BF = jnp.bfloat16
F32 = jnp.float32
I32 = jnp.int32


def sine_poly(t):
    s = t * t
    value = jnp.full_like(s, SINE[-1])
    for c in SINE[-2::-1]:
        value = value * s + c
    return value * t


def cos_sin(products):
    turns = products * (1.0 / GRID)
    frac = turns - jnp.floor(turns + 0.5)
    size = jnp.abs(frac)
    shifted = 0.25 - size
    cosine = sine_poly(shifted)
    folded = 0.25 - jnp.abs(shifted)
    sine = sine_poly(jnp.where(frac < 0.0, -folded, folded))
    return cosine, sine


def find_requests(owner_ref, row_ref, request_ref, slot_ref):
    before = (lax.broadcasted_iota(I32, (K, K), 0) < lax.broadcasted_iota(I32, (K, K), 1)).astype(F32).astype(BF)
    total = jnp.zeros((N_RE, LANES), F32)
    for q in range(Q):
        owner = owner_ref[q]
        row = row_ref[q : q + 1, :]
        hit = lax.broadcasted_iota(I32, (N_RE, K), 0) == owner
        one_hot = hit.astype(F32)
        earlier = jnp.dot(one_hot.astype(BF), before, preferred_element_type=F32)
        rank = jnp.sum(one_hot * earlier, axis=0, keepdims=True).astype(I32)
        slot_ref[q : q + 1, :] = owner * CAP + rank
        place = (lax.broadcasted_iota(I32, (LANES, K), 0) == rank + q * CAP).astype(F32).astype(BF)
        high = (one_hot * (row >> 4).astype(F32)).astype(BF)
        low = (one_hot * (row & 15).astype(F32)).astype(BF)
        contract = (((1,), (1,)), ((), ()))
        total += 16.0 * lax.dot_general(high, place, contract, preferred_element_type=F32)
        total += lax.dot_general(low, place, contract, preferred_element_type=F32)
    total = total.astype(I32)
    for o in range(N_RE):
        request_ref[o] = total[o : o + 1, :]


def mix_kernel(
    mode_ref, q_ref, rank_ref, rp_ref, owner_ref, row_ref, table_ref,
    own_ref, one_ref, two_ref, three_ref, request_ref, slot_ref,
):
    out_refs = own_ref, one_ref, two_ref, three_ref

    @pl.when(pl.program_id(0) == 0)
    def _():
        find_requests(owner_ref, row_ref, request_ref, slot_ref)

    group = 8
    width = group * RP_LOCAL
    coords = jnp.concatenate([rp_ref[...]] * group, axis=1)
    lane_group = lax.broadcasted_iota(I32, (group, width), 1) // RP_LOCAL
    own = lane_group == lax.broadcasted_iota(I32, (group, width), 0)
    cosines, sines = [], []
    for q in range(Q):
        products = sum(q_ref[q, d] * coords[d : d + 1, :] for d in range(3)).astype(F32)
        cosine, sine = cos_sin(jnp.broadcast_to(products, (group, width)))
        cosines.append(jnp.where(own, cosine, 0.0))
        sines.append(jnp.where(own, sine, 0.0))
    left = jnp.concatenate(cosines + sines, axis=0).astype(BF)
    half = MODES * NB * NB
    low_lanes = lax.broadcasted_iota(I32, (group, LANES), 1) < LANES // 2
    rank = rank_ref[0]
    parts = [[[] for _ in range(Q * M_LOCAL)] for _ in range(N_RP)]
    for h in range(table_ref.shape[0] // group):
        values = table_ref[h * group : (h + 1) * group].reshape(width, 2 * half)
        sums = jnp.dot(left, values, preferred_element_type=F32)
        for q in range(Q):
            with_cos = sums[q * group : (q + 1) * group]
            with_sin = sums[(Q + q) * group : (Q + q + 1) * group]
            packed = []
            for p in range(MODES // 2):
                re_lanes = slice(p * LANES, (p + 1) * LANES)
                im_lanes = slice(half + p * LANES, half + (p + 1) * LANES)
                real = with_cos[:, re_lanes] - with_sin[:, im_lanes]
                imag = with_sin[:, re_lanes] + with_cos[:, im_lanes]
                packed.append(jnp.where(low_lanes, real, pltpu.roll(imag, LANES // 2, 1)))
                packed.append(jnp.where(low_lanes, pltpu.roll(real, LANES // 2, 1), imag))
            for s in range(N_RP):
                first = (rank ^ s) * M_LOCAL
                for n in range(M_LOCAL):
                    value = mode_ref[0, q, first + n] * packed[0]
                    for mu in range(1, MODES):
                        value += mode_ref[mu, q, first + n] * packed[mu]
                    parts[s][q * M_LOCAL + n].append(value)
    for s in range(N_RP):
        for i in range(Q * M_LOCAL):
            out_refs[s][i] = jnp.concatenate(parts[s][i], axis=0).astype(BF)


def sum_kernel(own_ref, one_ref, two_ref, three_ref, out_hbm, total_ref, sem):
    total = own_ref[...].astype(F32) + one_ref[...].astype(F32)
    total += two_ref[...].astype(F32) + three_ref[...].astype(F32)
    total_ref[...] = total.astype(BF)
    copies = [pltpu.make_async_copy(total_ref, out_hbm.at[p, :ROWS, :], sem.at[p]) for p in range(N_RE)]
    for copy in copies:
        copy.start()
    for copy in copies:
        copy.wait()


def lookup_kernel(packed_ref, request_ref, rotations_ref, out_ref):
    peers = out_ref.shape[0]
    wanted = request_ref[:, 0, :].T
    rows = lax.broadcasted_iota(I32, (SLOTS, K), 1)
    one_hot = [(wanted[:SLOTS, p : p + 1] == rows).astype(F32).astype(BF) for p in range(peers)]
    found = jnp.dot(jnp.concatenate(one_hot, axis=0), rotations_ref[...], preferred_element_type=F32)
    out_ref[...] = found.reshape(peers, SLOTS, LANES).astype(BF)


def phase_kernel(re_ref, k_ref, out_ref):
    left = re_ref[...].astype(F32).astype(BF)
    for t in range(out_ref.shape[0]):
        right = k_ref[:, t * LANES : (t + 1) * LANES].astype(F32).astype(BF)
        products = lax.dot_general(left, right, (((0,), (0,)), ((), ())), preferred_element_type=F32)
        cosine, sine = cos_sin(products)
        out_ref[t, :, :LANES] = cosine.astype(BF)
        out_ref[t, :, LANES:] = sine.astype(BF)


def chain(terms):
    total = None
    for term in terms:
        total = term if total is None else total + term
    return total


def rotate(coupling_ref, far_ref, near_ref, out_ref, q, i, t):
    lanes = slice(t * LANES, (t + 1) * LANES)
    near = [[near_ref[o * SIZE + b * NB : o * SIZE + (b + 1) * NB, lanes] for b in range(NB)] for o in range(3)]
    halves = []
    for a in range(NB):
        real, imag, both = [
            chain(coupling_ref[o * SIZE + a * NB + b : o * SIZE + a * NB + b + 1] * near[o][b] for b in range(NB))
            for o in range(3)
        ]
        half = real - imag, both - (real + imag)
        halves.append((*half, half[0] + half[1]))
    for pair in range(NB // 2):
        results = [], []
        for m in (2 * pair, 2 * pair + 1):
            real, imag, both = [
                chain(far_ref[q, o * SIZE + a * NB + m : o * SIZE + a * NB + m + 1, lanes] * halves[a][o] for a in range(NB))
                for o in range(3)
            ]
            results[0].append(real + imag)
            results[1].append(both - (real - imag))
        rows = slice(pair * 2 * NB, (pair + 1) * 2 * NB)
        for c in range(2):
            out_ref[t, i, c, rows] = jnp.concatenate(results[c], axis=0).astype(BF)


def final_kernel(
    slot_ref, rotations_ref, first_ref, later_hbm, gathered_ref, out_hbm,
    later_ref, near_ref, turned_ref, far_ref, coupling_ref, out_ref, later_sem, out_sem,
):
    later = [pltpu.make_async_copy(later_hbm.at[t], later_ref.at[t], later_sem.at[t]) for t in range(TILES - FIRST)]
    out_copies = [
        pltpu.make_async_copy(out_ref.at[t], out_hbm.at[:, :, :, t * LANES : (t + 1) * LANES], out_sem.at[t])
        for t in range(TILES)
    ]
    for copy in later:
        copy.start()
    near = rotations_ref[...].astype(F32).T
    near_ref[: 2 * SIZE] = near
    near_ref[2 * SIZE :] = near[:SIZE] + near[SIZE:]
    replies = gathered_ref[:, ROWS:, :].astype(F32)
    place = lax.broadcasted_iota(I32, (N_RE * CAP, K), 0)
    for q in range(Q):
        rows = replies[:, q * CAP : (q + 1) * CAP, :].reshape(N_RE * CAP, LANES)
        one_hot = (place == slot_ref[q : q + 1, :]).astype(F32).astype(BF)
        far = jnp.dot(rows.T.astype(BF), one_hot, preferred_element_type=F32)
        far_ref[q, : 2 * SIZE] = far
        far_ref[q, 2 * SIZE :] = far[:SIZE] - far[SIZE:]
    for i in range(Q * M_LOCAL):
        block = gathered_ref[:, i * RE_LOCAL : (i + 1) * RE_LOCAL, :].reshape(RE, LANES)
        turned_ref[i] = block.T

    def couple(t, i):
        phase = first_ref[t] if t < FIRST else later_ref[t - FIRST]
        both = jnp.dot(turned_ref[i], phase, preferred_element_type=F32)
        real = both[:SIZE, :LANES] - both[SIZE:, LANES:]
        imag = both[:SIZE, LANES:] + both[SIZE:, :LANES]
        coupling_ref[t % 2, i, :SIZE] = real
        coupling_ref[t % 2, i, SIZE : 2 * SIZE] = imag
        coupling_ref[t % 2, i, 2 * SIZE :] = real + imag

    for i in range(Q * M_LOCAL):
        couple(0, i)
    for t in range(TILES):
        if FIRST <= t + 1 < TILES:
            later[t + 1 - FIRST].wait()
        for i in range(Q * M_LOCAL):
            if t + 1 < TILES:
                couple(t + 1, i)
            rotate(coupling_ref.at[t % 2, i], far_ref, near_ref, out_ref, i // M_LOCAL, i, t)
        out_copies[t].start()
    for t in range(TILES):
        out_copies[t].wait()


def whole(shape):
    return pl.BlockSpec(shape, lambda *_: (0,) * len(shape))


def smem():
    return pl.BlockSpec(memory_space=pltpu.SMEM)


def in_hbm(array):
    return pltpu.with_memory_space_constraint(array, pltpu.HBM)


def params(mebibytes):
    return pltpu.CompilerParams(vmem_limit_bytes=mebibytes << 20)


def local(
    wannier_table,
    mode_matrix,
    re_coords,
    rp_coords,
    q_coords,
    k_coords,
    rotations,
    kq_owner,
    kq_row,
):
    hbm = pl.BlockSpec(memory_space=pltpu.HBM)
    vmem = pl.BlockSpec(memory_space=pltpu.VMEM)
    part = pl.BlockSpec((Q * M_LOCAL, CHUNK, LANES), lambda i: (0, i, 0))
    *parts, requests, slots = pl.pallas_call(
        mix_kernel,
        grid=(RE_LOCAL // CHUNK,),
        in_specs=[
            smem(),
            smem(),
            smem(),
            whole((3, RP_LOCAL)),
            whole((Q, 1, K)),
            whole((Q, K)),
            pl.BlockSpec((CHUNK, RP_LOCAL, 2 * MODES * SIZE), lambda i: (i, 0, 0)),
        ],
        out_specs=[part] * N_RP + [whole((N_RE, 1, LANES)), whole((Q, K))],
        out_shape=[jax.ShapeDtypeStruct((Q * M_LOCAL, RE_LOCAL, LANES), BF)] * N_RP
        + [jax.ShapeDtypeStruct((N_RE, 1, LANES), I32), jax.ShapeDtypeStruct((Q, K), I32)],
        compiler_params=params(16),
        name="mix",
    )(
        in_hbm(mode_matrix.transpose(1, 0, 2)),
        in_hbm(q_coords.T),
        lax.axis_index("rp").reshape(1),
        in_hbm(rp_coords),
        in_hbm(kq_owner.transpose(0, 2, 1)),
        in_hbm(kq_row),
        in_hbm(wannier_table),
    )
    own = parts[0].reshape(ROWS, LANES)
    others = [
        lax.ppermute(parts[s].reshape(ROWS, LANES), "rp", [(j, j ^ s) for j in range(N_RP)])
        for s in range(1, N_RP)
    ]

    wanted = lax.all_to_all(requests, "re", split_axis=0, concat_axis=0, tiled=True)

    spread = pl.pallas_call(
        sum_kernel,
        in_specs=[vmem] * N_RP,
        out_specs=hbm,
        out_shape=pltpu.HBM((N_RE, PACK, LANES), BF),
        scratch_shapes=[pltpu.VMEM((ROWS, LANES), BF), pltpu.SemaphoreType.DMA((N_RE,))],
        compiler_params=params(8),
        name="sum",
    )(own, *others)
    packed = pl.pallas_call(
        lookup_kernel,
        grid=(1,),
        in_specs=[
            pl.BlockSpec(memory_space=pltpu.HBM),
            pl.BlockSpec(memory_space=pltpu.VMEM),
            pl.BlockSpec(memory_space=pltpu.VMEM),
        ],
        out_specs=pl.BlockSpec((N_RE, SLOTS, LANES), lambda i: (0, ROWS // SLOTS, 0)),
        out_shape=pltpu.HBM((N_RE, PACK, LANES), BF),
        input_output_aliases={0: 0},
        compiler_params=params(8),
        name="lookup",
    )(spread, wanted, rotations)
    gathered = lax.all_to_all(packed, "re", split_axis=0, concat_axis=0, tiled=True)

    def phase_tiles(coords, space):
        tiles = coords.shape[1] // LANES
        return pl.pallas_call(
            phase_kernel,
            out_shape=space((tiles, RE, 2 * LANES), BF),
            compiler_params=params(16),
            name="phase",
        )(in_hbm(re_coords), in_hbm(coords))

    first = phase_tiles(k_coords[:, : FIRST * LANES], pltpu.VMEM)
    later = phase_tiles(k_coords[:, FIRST * LANES :], pltpu.HBM)

    result = pl.pallas_call(
        final_kernel,
        in_specs=[vmem, vmem, vmem, hbm, vmem],
        out_specs=hbm,
        out_shape=jax.ShapeDtypeStruct((Q * M_LOCAL, 2, SIZE, K), BF),
        scratch_shapes=[
            pltpu.VMEM((TILES - FIRST, RE, 2 * LANES), BF),
            pltpu.VMEM((3 * SIZE, K), F32),
            pltpu.VMEM((Q * M_LOCAL, LANES, RE), BF),
            pltpu.VMEM((Q, 3 * SIZE, K), F32),
            pltpu.VMEM((2, Q * M_LOCAL, 3 * SIZE, LANES), F32),
            pltpu.VMEM((TILES, Q * M_LOCAL, 2, SIZE, LANES), BF),
            pltpu.SemaphoreType.DMA((TILES - FIRST,)),
            pltpu.SemaphoreType.DMA((TILES,)),
        ],
        compiler_params=params(24),
        name="final",
    )(slots, rotations, first, in_hbm(later), gathered)
    return result.reshape(Q, M_LOCAL, 2, NB * NB, K)


def solution(mesh):
    in_specs = (
        P("re", "rp", None),
        P(),
        P(),
        P(None, "rp"),
        P(),
        P(None, "re"),
        P("re", None),
        P(None, "re", None),
        P(None, "re"),
    )
    out_specs = P(None, "rp", None, None, "re")
    return jax.shard_map(local, mesh=mesh, in_specs=in_specs, out_specs=out_specs, check_vma=False)
```

```python
import math

import jax
import jax.numpy as jnp
from jax import lax
from jax.experimental import pallas as pl
from jax.experimental.pallas import tpu as pltpu
from jax.sharding import PartitionSpec as P

NB = 8
MODES = 12
Q = 2
GRID = 64
RE = 1024
RE_LOCAL = 32
RP_LOCAL = 32
K = 512
N_RE = 32
N_RP = 4
M_LOCAL = MODES // N_RP
CAP = 24
ROWS = Q * M_LOCAL * RE_LOCAL
PACK = ROWS + CAP
LANES = 128
TILES = K // LANES
FIRST = 2
CHUNK = 16
SIZE = NB * NB
TURN = 2.0 * math.pi
SINE = [TURN ** n * s / math.factorial(n) for n, s in ((1, 1), (3, -1), (5, 1), (7, -1), (9, 1), (11, -1))]
BF = jnp.bfloat16
F32 = jnp.float32
I32 = jnp.int32


def sine_poly(t):
    s = t * t
    value = jnp.full_like(s, SINE[-1])
    for c in SINE[-2::-1]:
        value = value * s + c
    return value * t


def cos_sin(products):
    turns = products * (1.0 / GRID)
    frac = turns - jnp.floor(turns + 0.5)
    size = jnp.abs(frac)
    shifted = 0.25 - size
    cosine = sine_poly(shifted)
    folded = 0.25 - jnp.abs(shifted)
    sine = sine_poly(jnp.where(frac < 0.0, -folded, folded))
    return cosine, sine


def find_requests(q, owner_ref, row_ref, request_ref, slot_ref):
    before = (lax.broadcasted_iota(I32, (K, K), 0) < lax.broadcasted_iota(I32, (K, K), 1)).astype(F32).astype(BF)
    owner = owner_ref[q]
    row = row_ref[pl.ds(q, 1), :]
    one_hot = (lax.broadcasted_iota(I32, (N_RE, K), 0) == owner).astype(F32)
    earlier = jnp.dot(one_hot.astype(BF), before, preferred_element_type=F32)
    rank = jnp.sum(one_hot * earlier, axis=0, keepdims=True).astype(I32)
    slot_ref[...] = owner * CAP + rank
    place = (lax.broadcasted_iota(I32, (LANES, K), 0) == rank).astype(F32).astype(BF)
    high = (one_hot * (row >> 4).astype(F32)).astype(BF)
    low = (one_hot * (row & 15).astype(F32)).astype(BF)
    contract = (((1,), (1,)), ((), ()))
    total = 16.0 * lax.dot_general(high, place, contract, preferred_element_type=F32)
    total += lax.dot_general(low, place, contract, preferred_element_type=F32)
    total = total.astype(I32)
    for o in range(N_RE):
        request_ref[o] = total[o : o + 1, :]


def mix_kernel(
    mode_ref, q_ref, rank_ref, rp_ref, owner_ref, row_ref, table_ref,
    own_ref, one_ref, two_ref, three_ref, request_ref, slot_ref,
):
    out_refs = own_ref, one_ref, two_ref, three_ref

    @pl.when(pl.program_id(0) == 0)
    def _():
        find_requests(rank_ref[0] % Q, owner_ref, row_ref, request_ref, slot_ref)

    group = 8
    width = group * RP_LOCAL
    coords = jnp.concatenate([rp_ref[...]] * group, axis=1)
    lane_group = lax.broadcasted_iota(I32, (group, width), 1) // RP_LOCAL
    own = lane_group == lax.broadcasted_iota(I32, (group, width), 0)
    cosines, sines = [], []
    for q in range(Q):
        products = sum(q_ref[q, d] * coords[d : d + 1, :] for d in range(3)).astype(F32)
        cosine, sine = cos_sin(jnp.broadcast_to(products, (group, width)))
        cosines.append(jnp.where(own, cosine, 0.0))
        sines.append(jnp.where(own, sine, 0.0))
    left = jnp.concatenate(cosines + sines, axis=0).astype(BF)
    half = MODES * NB * NB
    low_lanes = lax.broadcasted_iota(I32, (group, LANES), 1) < LANES // 2
    rank = rank_ref[0]
    parts = [[[] for _ in range(Q * M_LOCAL)] for _ in range(N_RP)]
    for h in range(table_ref.shape[0] // group):
        values = table_ref[h * group : (h + 1) * group].reshape(width, 2 * half)
        sums = jnp.dot(left, values, preferred_element_type=F32)
        for q in range(Q):
            with_cos = sums[q * group : (q + 1) * group]
            with_sin = sums[(Q + q) * group : (Q + q + 1) * group]
            packed = []
            for p in range(MODES // 2):
                re_lanes = slice(p * LANES, (p + 1) * LANES)
                im_lanes = slice(half + p * LANES, half + (p + 1) * LANES)
                real = with_cos[:, re_lanes] - with_sin[:, im_lanes]
                imag = with_sin[:, re_lanes] + with_cos[:, im_lanes]
                packed.append(jnp.where(low_lanes, real, pltpu.roll(imag, LANES // 2, 1)))
                packed.append(jnp.where(low_lanes, pltpu.roll(real, LANES // 2, 1), imag))
            for s in range(N_RP):
                first = (rank ^ s) * M_LOCAL
                for n in range(M_LOCAL):
                    value = mode_ref[0, q, first + n] * packed[0]
                    for mu in range(1, MODES):
                        value += mode_ref[mu, q, first + n] * packed[mu]
                    parts[s][q * M_LOCAL + n].append(value)
    for s in range(N_RP):
        for i in range(Q * M_LOCAL):
            out_refs[s][i] = jnp.concatenate(parts[s][i], axis=0).astype(BF)


def sum_kernel(own_ref, one_ref, two_ref, three_ref, out_hbm, total_ref, sem):
    total = own_ref[...].astype(F32) + one_ref[...].astype(F32)
    total += two_ref[...].astype(F32) + three_ref[...].astype(F32)
    total_ref[...] = total.astype(BF)
    copies = [pltpu.make_async_copy(total_ref, out_hbm.at[p, :ROWS, :], sem.at[p]) for p in range(N_RE)]
    for copy in copies:
        copy.start()
    for copy in copies:
        copy.wait()


def lookup_kernel(packed_ref, request_ref, rotations_ref, out_ref):
    wanted = request_ref[:, 0, :].T
    rows = lax.broadcasted_iota(I32, (CAP, K), 1)
    one_hot = [(wanted[:CAP, p : p + 1] == rows).astype(F32) for p in range(N_RE)]
    one_hot = jnp.concatenate(one_hot, axis=0).astype(BF)
    found = jnp.dot(one_hot, rotations_ref[...], preferred_element_type=F32)
    out_ref[...] = found.reshape(N_RE, CAP, LANES).astype(BF)


def phase_kernel(re_ref, k_ref, out_ref):
    left = re_ref[...].astype(F32).astype(BF)
    for t in range(out_ref.shape[0]):
        right = k_ref[:, t * LANES : (t + 1) * LANES].astype(F32).astype(BF)
        products = lax.dot_general(left, right, (((0,), (0,)), ((), ())), preferred_element_type=F32)
        cosine, sine = cos_sin(products)
        out_ref[t, :, :LANES] = cosine.astype(BF)
        out_ref[t, :, LANES:] = sine.astype(BF)


def chain(terms):
    total = None
    for term in terms:
        total = term if total is None else total + term
    return total


def rotate(coupling_ref, far_ref, near_ref, out_ref, q, i, t):
    lanes = slice(t * LANES, (t + 1) * LANES)
    near = [[near_ref[o * SIZE + b * NB : o * SIZE + (b + 1) * NB, lanes] for b in range(NB)] for o in range(3)]
    halves = []
    for a in range(NB):
        real, imag, both = [
            chain(coupling_ref[o * SIZE + a * NB + b : o * SIZE + a * NB + b + 1] * near[o][b] for b in range(NB))
            for o in range(3)
        ]
        half = real - imag, both - (real + imag)
        halves.append((*half, half[0] + half[1]))
    for pair in range(NB // 2):
        results = [], []
        for m in (2 * pair, 2 * pair + 1):
            real, imag, both = [
                chain(far_ref[q, o * SIZE + a * NB + m : o * SIZE + a * NB + m + 1, lanes] * halves[a][o] for a in range(NB))
                for o in range(3)
            ]
            results[0].append(real + imag)
            results[1].append(both - (real - imag))
        rows = slice(pair * 2 * NB, (pair + 1) * 2 * NB)
        for c in range(2):
            out_ref[t, i, c, rows] = jnp.concatenate(results[c], axis=0).astype(BF)


def far_kernel(slot_ref, gathered_ref, out_ref):
    replies = gathered_ref[:, ROWS:, :].astype(F32).reshape(N_RE * CAP, LANES)
    place = lax.broadcasted_iota(I32, (N_RE * CAP, K), 0)
    one_hot = (place == slot_ref[...]).astype(F32).astype(BF)
    out_ref[...] = jnp.dot(replies.T.astype(BF), one_hot, preferred_element_type=F32).astype(BF)


def couple_kernel(first_ref, later_hbm, gathered_ref, out_ref, later_ref, turned_ref, later_sem):
    later = [pltpu.make_async_copy(later_hbm.at[t], later_ref.at[t], later_sem.at[t]) for t in range(TILES - FIRST)]
    for copy in later:
        copy.start()
    for i in range(Q * M_LOCAL):
        block = gathered_ref[:, i * RE_LOCAL : (i + 1) * RE_LOCAL, :].reshape(RE, LANES)
        turned_ref[i] = block.T
    for t in range(TILES):
        if t >= FIRST:
            later[t - FIRST].wait()
        for i in range(Q * M_LOCAL):
            phase = first_ref[t] if t < FIRST else later_ref[t - FIRST]
            both = jnp.dot(turned_ref[i], phase, preferred_element_type=F32)
            real = both[:SIZE, :LANES] - both[SIZE:, LANES:]
            imag = both[:SIZE, LANES:] + both[SIZE:, :LANES]
            out_ref[t, i, :SIZE] = real
            out_ref[t, i, SIZE : 2 * SIZE] = imag
            out_ref[t, i, 2 * SIZE :] = real + imag


def final_kernel(rank_ref, rotations_ref, mine_ref, mate_ref, coupling_ref, out_hbm, near_ref, far_ref, out_ref, out_sem):
    out_copies = [
        pltpu.make_async_copy(out_ref.at[t], out_hbm.at[:, :, :, t * LANES : (t + 1) * LANES], out_sem.at[t])
        for t in range(TILES)
    ]
    near = rotations_ref[...].astype(F32).T
    near_ref[: 2 * SIZE] = near
    near_ref[2 * SIZE :] = near[:SIZE] + near[SIZE:]
    mine = mine_ref[...].astype(F32)
    mate = mate_ref[...].astype(F32)
    for q in range(Q):
        far = jnp.where(rank_ref[0] % Q == q, mine, mate)
        far_ref[q, : 2 * SIZE] = far
        far_ref[q, 2 * SIZE :] = far[:SIZE] - far[SIZE:]
    for t in range(TILES):
        for i in range(Q * M_LOCAL):
            rotate(coupling_ref.at[t, i], far_ref, near_ref, out_ref, i // M_LOCAL, i, t)
        out_copies[t].start()
    for t in range(TILES):
        out_copies[t].wait()


def whole(shape):
    return pl.BlockSpec(shape, lambda *_: (0,) * len(shape))


def smem():
    return pl.BlockSpec(memory_space=pltpu.SMEM)


def in_hbm(array):
    return pltpu.with_memory_space_constraint(array, pltpu.HBM)


def params(mebibytes):
    return pltpu.CompilerParams(vmem_limit_bytes=mebibytes << 20)


def local(
    wannier_table,
    mode_matrix,
    re_coords,
    rp_coords,
    q_coords,
    k_coords,
    rotations,
    kq_owner,
    kq_row,
):
    hbm = pl.BlockSpec(memory_space=pltpu.HBM)
    vmem = pl.BlockSpec(memory_space=pltpu.VMEM)
    rank = lax.axis_index("rp").reshape(1)
    part = pl.BlockSpec((Q * M_LOCAL, CHUNK, LANES), lambda i: (0, i, 0))
    *parts, requests, slots = pl.pallas_call(
        mix_kernel,
        grid=(RE_LOCAL // CHUNK,),
        in_specs=[
            smem(),
            smem(),
            smem(),
            whole((3, RP_LOCAL)),
            whole((Q, 1, K)),
            whole((Q, K)),
            pl.BlockSpec((CHUNK, RP_LOCAL, 2 * MODES * SIZE), lambda i: (i, 0, 0)),
        ],
        out_specs=[part] * N_RP + [whole((N_RE, 1, LANES)), whole((1, K))],
        out_shape=[jax.ShapeDtypeStruct((Q * M_LOCAL, RE_LOCAL, LANES), BF)] * N_RP
        + [jax.ShapeDtypeStruct((N_RE, 1, LANES), I32), jax.ShapeDtypeStruct((1, K), I32)],
        compiler_params=params(16),
        name="mix",
    )(
        in_hbm(mode_matrix.transpose(1, 0, 2)),
        in_hbm(q_coords.T),
        rank,
        in_hbm(rp_coords),
        in_hbm(kq_owner.transpose(0, 2, 1)),
        in_hbm(kq_row),
        in_hbm(wannier_table),
    )
    own = parts[0].reshape(ROWS, LANES)
    others = [
        lax.ppermute(parts[s].reshape(ROWS, LANES), "rp", [(j, j ^ s) for j in range(N_RP)])
        for s in range(1, N_RP)
    ]

    wanted = lax.all_to_all(requests, "re", split_axis=0, concat_axis=0, tiled=True)

    spread = pl.pallas_call(
        sum_kernel,
        in_specs=[vmem] * N_RP,
        out_specs=hbm,
        out_shape=pltpu.HBM((N_RE, PACK, LANES), BF),
        scratch_shapes=[pltpu.VMEM((ROWS, LANES), BF), pltpu.SemaphoreType.DMA((N_RE,))],
        compiler_params=params(8),
        name="sum",
    )(own, *others)
    packed = pl.pallas_call(
        lookup_kernel,
        grid=(1,),
        in_specs=[
            pl.BlockSpec(memory_space=pltpu.HBM),
            pl.BlockSpec(memory_space=pltpu.VMEM),
            pl.BlockSpec(memory_space=pltpu.VMEM),
        ],
        out_specs=pl.BlockSpec((N_RE, CAP, LANES), lambda i: (0, ROWS // CAP, 0)),
        out_shape=pltpu.HBM((N_RE, PACK, LANES), BF),
        input_output_aliases={0: 0},
        compiler_params=params(8),
        name="lookup",
    )(spread, wanted, rotations)
    gathered = lax.all_to_all(packed, "re", split_axis=0, concat_axis=0, tiled=True)

    def phase_tiles(coords, space):
        tiles = coords.shape[1] // LANES
        return pl.pallas_call(
            phase_kernel,
            out_shape=space((tiles, RE, 2 * LANES), BF),
            compiler_params=params(16),
            name="phase",
        )(in_hbm(re_coords), in_hbm(coords))

    first = phase_tiles(k_coords[:, : FIRST * LANES], pltpu.VMEM)
    later = phase_tiles(k_coords[:, FIRST * LANES :], pltpu.HBM)

    slots, first, later = lax.optimization_barrier((slots, first, later))
    far = pl.pallas_call(
        far_kernel,
        in_specs=[vmem, vmem],
        out_shape=jax.ShapeDtypeStruct((LANES, K), BF),
        compiler_params=params(16),
        name="far",
    )(slots, gathered)
    mate = lax.ppermute(far, "rp", [(j, j ^ 1) for j in range(N_RP)])
    coupling = pl.pallas_call(
        couple_kernel,
        in_specs=[vmem, hbm, vmem],
        out_shape=pltpu.VMEM((TILES, Q * M_LOCAL, 3 * SIZE, LANES), F32),
        scratch_shapes=[
            pltpu.VMEM((TILES - FIRST, RE, 2 * LANES), BF),
            pltpu.VMEM((Q * M_LOCAL, LANES, RE), BF),
            pltpu.SemaphoreType.DMA((TILES - FIRST,)),
        ],
        compiler_params=params(16),
        name="couple",
    )(first, in_hbm(later), gathered)
    result = pl.pallas_call(
        final_kernel,
        in_specs=[smem(), vmem, vmem, vmem, vmem],
        out_specs=hbm,
        out_shape=jax.ShapeDtypeStruct((Q * M_LOCAL, 2, SIZE, K), BF),
        scratch_shapes=[
            pltpu.VMEM((3 * SIZE, K), F32),
            pltpu.VMEM((Q, 3 * SIZE, K), F32),
            pltpu.VMEM((TILES, Q * M_LOCAL, 2, SIZE, LANES), BF),
            pltpu.SemaphoreType.DMA((TILES,)),
        ],
        compiler_params=params(16),
        name="final",
    )(rank, rotations, far, mate, coupling)
    return result.reshape(Q, M_LOCAL, 2, NB * NB, K)


def solution(mesh):
    in_specs = (
        P("re", "rp", None),
        P(),
        P(),
        P(None, "rp"),
        P(),
        P(None, "re"),
        P("re", None),
        P(None, "re", None),
        P(None, "re"),
    )
    out_specs = P(None, "rp", None, None, "re")
    return jax.shard_map(local, mesh=mesh, in_specs=in_specs, out_specs=out_specs, check_vma=False)
```

```python
import math

import jax
import jax.numpy as jnp
from jax import lax
from jax.experimental import pallas as pl
from jax.experimental.pallas import tpu as pltpu
from jax.sharding import PartitionSpec as P

NB = 8
MODES = 12
Q = 2
GRID = 64
RE = 1024
RE_LOCAL = 32
RP_LOCAL = 32
K = 512
N_RE = 32
N_RP = 4
M_LOCAL = MODES // N_RP
CAP = 24
ROWS = Q * M_LOCAL * RE_LOCAL
PACK = ROWS + CAP
LANES = 128
TILES = K // LANES
FIRST = 2
CHUNK = 16
SIZE = NB * NB
TURN = 2.0 * math.pi
SINE = [TURN ** n * s / math.factorial(n) for n, s in ((1, 1), (3, -1), (5, 1), (7, -1), (9, 1), (11, -1))]
BF = jnp.bfloat16
F32 = jnp.float32
I32 = jnp.int32


def sine_poly(t):
    s = t * t
    value = jnp.full_like(s, SINE[-1])
    for c in SINE[-2::-1]:
        value = value * s + c
    return value * t


def cos_sin(products):
    turns = products * (1.0 / GRID)
    frac = turns - jnp.floor(turns + 0.5)
    size = jnp.abs(frac)
    shifted = 0.25 - size
    cosine = sine_poly(shifted)
    folded = 0.25 - jnp.abs(shifted)
    sine = sine_poly(jnp.where(frac < 0.0, -folded, folded))
    return cosine, sine


def find_requests(q, owner_ref, row_ref, request_ref, slot_ref):
    before = (lax.broadcasted_iota(I32, (K, K), 0) < lax.broadcasted_iota(I32, (K, K), 1)).astype(F32).astype(BF)
    owner = owner_ref[q]
    row = row_ref[pl.ds(q, 1), :]
    one_hot = (lax.broadcasted_iota(I32, (N_RE, K), 0) == owner).astype(F32)
    earlier = jnp.dot(one_hot.astype(BF), before, preferred_element_type=F32)
    rank = jnp.sum(one_hot * earlier, axis=0, keepdims=True).astype(I32)
    slot_ref[...] = owner * CAP + rank
    place = (lax.broadcasted_iota(I32, (LANES, K), 0) == rank).astype(F32).astype(BF)
    high = (one_hot * (row >> 4).astype(F32)).astype(BF)
    low = (one_hot * (row & 15).astype(F32)).astype(BF)
    contract = (((1,), (1,)), ((), ()))
    total = 16.0 * lax.dot_general(high, place, contract, preferred_element_type=F32)
    total += lax.dot_general(low, place, contract, preferred_element_type=F32)
    total = total.astype(I32)
    for o in range(N_RE):
        request_ref[o] = total[o : o + 1, :]


def mix_kernel(
    mode_ref, q_ref, rank_ref, rp_ref, owner_ref, row_ref, table_ref,
    own_ref, one_ref, two_ref, three_ref, request_ref, slot_ref,
):
    out_refs = own_ref, one_ref, two_ref, three_ref

    @pl.when(pl.program_id(0) == 0)
    def _():
        find_requests(rank_ref[0] % Q, owner_ref, row_ref, request_ref, slot_ref)

    group = 8
    width = group * RP_LOCAL
    coords = jnp.concatenate([rp_ref[...]] * group, axis=1)
    lane_group = lax.broadcasted_iota(I32, (group, width), 1) // RP_LOCAL
    own = lane_group == lax.broadcasted_iota(I32, (group, width), 0)
    cosines, sines = [], []
    for q in range(Q):
        products = sum(q_ref[q, d] * coords[d : d + 1, :] for d in range(3)).astype(F32)
        cosine, sine = cos_sin(jnp.broadcast_to(products, (group, width)))
        cosines.append(jnp.where(own, cosine, 0.0))
        sines.append(jnp.where(own, sine, 0.0))
    left = jnp.concatenate(cosines + sines, axis=0).astype(BF)
    half = MODES * NB * NB
    low_lanes = lax.broadcasted_iota(I32, (group, LANES), 1) < LANES // 2
    rank = rank_ref[0]
    parts = [[[] for _ in range(Q * M_LOCAL)] for _ in range(N_RP)]
    for h in range(table_ref.shape[0] // group):
        values = table_ref[h * group : (h + 1) * group].reshape(width, 2 * half)
        sums = jnp.dot(left, values, preferred_element_type=F32)
        for q in range(Q):
            with_cos = sums[q * group : (q + 1) * group]
            with_sin = sums[(Q + q) * group : (Q + q + 1) * group]
            packed = []
            for p in range(MODES // 2):
                re_lanes = slice(p * LANES, (p + 1) * LANES)
                im_lanes = slice(half + p * LANES, half + (p + 1) * LANES)
                real = with_cos[:, re_lanes] - with_sin[:, im_lanes]
                imag = with_sin[:, re_lanes] + with_cos[:, im_lanes]
                packed.append(jnp.where(low_lanes, real, pltpu.roll(imag, LANES // 2, 1)))
                packed.append(jnp.where(low_lanes, pltpu.roll(real, LANES // 2, 1), imag))
            for s in range(N_RP):
                first = (rank ^ s) * M_LOCAL
                for n in range(M_LOCAL):
                    value = mode_ref[0, q, first + n] * packed[0]
                    for mu in range(1, MODES):
                        value += mode_ref[mu, q, first + n] * packed[mu]
                    parts[s][q * M_LOCAL + n].append(value)
    for s in range(N_RP):
        for i in range(Q * M_LOCAL):
            out_refs[s][i] = jnp.concatenate(parts[s][i], axis=0).astype(BF)


def sum_kernel(own_ref, one_ref, two_ref, three_ref, out_hbm, total_ref, sem):
    total = own_ref[...].astype(F32) + one_ref[...].astype(F32)
    total += two_ref[...].astype(F32) + three_ref[...].astype(F32)
    total_ref[...] = total.astype(BF)
    copies = [pltpu.make_async_copy(total_ref, out_hbm.at[p, :ROWS, :], sem.at[p]) for p in range(N_RE)]
    for copy in copies:
        copy.start()
    for copy in copies:
        copy.wait()


def lookup_kernel(packed_ref, request_ref, rotations_ref, out_ref):
    wanted = request_ref[:, 0, :].T
    rows = lax.broadcasted_iota(I32, (CAP, K), 1)
    one_hot = [(wanted[:CAP, p : p + 1] == rows).astype(F32) for p in range(N_RE)]
    one_hot = jnp.concatenate(one_hot, axis=0).astype(BF)
    found = jnp.dot(one_hot, rotations_ref[...], preferred_element_type=F32)
    out_ref[...] = found.reshape(N_RE, CAP, LANES).astype(BF)


def phase_kernel(re_ref, k_ref, out_ref):
    left = re_ref[...].astype(F32).astype(BF)
    for t in range(out_ref.shape[0]):
        right = k_ref[:, t * LANES : (t + 1) * LANES].astype(F32).astype(BF)
        products = lax.dot_general(left, right, (((0,), (0,)), ((), ())), preferred_element_type=F32)
        cosine, sine = cos_sin(products)
        out_ref[t, :, :LANES] = cosine.astype(BF)
        out_ref[t, :, LANES:] = sine.astype(BF)


def chain(terms):
    total = None
    for term in terms:
        total = term if total is None else total + term
    return total


def rotate(coupling_ref, far_ref, near_ref, out_ref, q, i, t):
    lanes = slice(t * LANES, (t + 1) * LANES)
    near = [[near_ref[o * SIZE + b * NB : o * SIZE + (b + 1) * NB, lanes] for b in range(NB)] for o in range(3)]
    halves = []
    for a in range(NB):
        real, imag, both = [
            chain(coupling_ref[o * SIZE + a * NB + b : o * SIZE + a * NB + b + 1] * near[o][b] for b in range(NB))
            for o in range(3)
        ]
        half = real - imag, both - (real + imag)
        halves.append((*half, half[0] + half[1]))
    for pair in range(NB // 2):
        results = [], []
        for m in (2 * pair, 2 * pair + 1):
            real, imag, both = [
                chain(far_ref[q, o * SIZE + a * NB + m : o * SIZE + a * NB + m + 1, lanes] * halves[a][o] for a in range(NB))
                for o in range(3)
            ]
            results[0].append(real + imag)
            results[1].append(both - (real - imag))
        rows = slice(pair * 2 * NB, (pair + 1) * 2 * NB)
        for c in range(2):
            out_ref[t, i, c, rows] = jnp.concatenate(results[c], axis=0).astype(BF)


def far_kernel(slot_ref, gathered_ref, out_ref):
    replies = gathered_ref[:, ROWS:, :].astype(F32).reshape(N_RE * CAP, LANES)
    place = lax.broadcasted_iota(I32, (N_RE * CAP, K), 0)
    one_hot = (place == slot_ref[...]).astype(F32).astype(BF)
    out_ref[...] = jnp.dot(replies.T.astype(BF), one_hot, preferred_element_type=F32).astype(BF)


def couple_kernel(first_ref, later_hbm, gathered_ref, out_ref, later_ref, turned_ref, later_sem):
    later = [pltpu.make_async_copy(later_hbm.at[t], later_ref.at[t], later_sem.at[t]) for t in range(TILES - FIRST)]
    for copy in later:
        copy.start()
    for i in range(Q * M_LOCAL):
        block = gathered_ref[:, i * RE_LOCAL : (i + 1) * RE_LOCAL, :].reshape(RE, LANES)
        turned_ref[i] = block.T
    for t in range(TILES):
        if t >= FIRST:
            later[t - FIRST].wait()
        for i in range(Q * M_LOCAL):
            phase = first_ref[t] if t < FIRST else later_ref[t - FIRST]
            both = jnp.dot(turned_ref[i], phase, preferred_element_type=F32)
            real = both[:SIZE, :LANES] - both[SIZE:, LANES:]
            imag = both[:SIZE, LANES:] + both[SIZE:, :LANES]
            out_ref[t, i, :SIZE] = real
            out_ref[t, i, SIZE : 2 * SIZE] = imag
            out_ref[t, i, 2 * SIZE :] = real + imag


def near_kernel(rotations_ref, near_ref):
    near = rotations_ref[...].astype(F32).T
    near_ref[: 2 * SIZE] = near
    near_ref[2 * SIZE :] = near[:SIZE] + near[SIZE:]


def final_kernel(rank_ref, near_ref, mine_ref, mate_ref, coupling_ref, out_hbm, far_ref, out_ref, out_sem):
    out_copies = [
        [
            pltpu.make_async_copy(
                out_ref.at[t, q * M_LOCAL : (q + 1) * M_LOCAL],
                out_hbm.at[q * M_LOCAL : (q + 1) * M_LOCAL, :, :, t * LANES : (t + 1) * LANES],
                out_sem.at[t, q],
            )
            for q in range(Q)
        ]
        for t in range(TILES)
    ]
    mine = mine_ref[...].astype(F32)
    mate = mate_ref[...].astype(F32)
    for q in range(Q):
        far = jnp.where(rank_ref[0] % Q == q, mine, mate)
        far_ref[q, : 2 * SIZE] = far
        far_ref[q, 2 * SIZE :] = far[:SIZE] - far[SIZE:]
    for t in range(TILES):
        for q in range(Q):
            for i in range(q * M_LOCAL, (q + 1) * M_LOCAL):
                rotate(coupling_ref.at[t, i], far_ref, near_ref, out_ref, q, i, t)
            out_copies[t][q].start()
    for t in range(TILES):
        for q in range(Q):
            out_copies[t][q].wait()


def whole(shape):
    return pl.BlockSpec(shape, lambda *_: (0,) * len(shape))


def smem():
    return pl.BlockSpec(memory_space=pltpu.SMEM)


def in_hbm(array):
    return pltpu.with_memory_space_constraint(array, pltpu.HBM)


def params(mebibytes):
    return pltpu.CompilerParams(vmem_limit_bytes=mebibytes << 20)


def local(
    wannier_table,
    mode_matrix,
    re_coords,
    rp_coords,
    q_coords,
    k_coords,
    rotations,
    kq_owner,
    kq_row,
):
    hbm = pl.BlockSpec(memory_space=pltpu.HBM)
    vmem = pl.BlockSpec(memory_space=pltpu.VMEM)
    rank = lax.axis_index("rp").reshape(1)
    part = pl.BlockSpec((Q * M_LOCAL, CHUNK, LANES), lambda i: (0, i, 0))
    *parts, requests, slots = pl.pallas_call(
        mix_kernel,
        grid=(RE_LOCAL // CHUNK,),
        in_specs=[
            smem(),
            smem(),
            smem(),
            whole((3, RP_LOCAL)),
            whole((Q, 1, K)),
            whole((Q, K)),
            pl.BlockSpec((CHUNK, RP_LOCAL, 2 * MODES * SIZE), lambda i: (i, 0, 0)),
        ],
        out_specs=[part] * N_RP + [whole((N_RE, 1, LANES)), whole((1, K))],
        out_shape=[jax.ShapeDtypeStruct((Q * M_LOCAL, RE_LOCAL, LANES), BF)] * N_RP
        + [jax.ShapeDtypeStruct((N_RE, 1, LANES), I32), jax.ShapeDtypeStruct((1, K), I32)],
        compiler_params=params(16),
        name="mix",
    )(
        in_hbm(mode_matrix.transpose(1, 0, 2)),
        in_hbm(q_coords.T),
        rank,
        in_hbm(rp_coords),
        in_hbm(kq_owner.transpose(0, 2, 1)),
        in_hbm(kq_row),
        in_hbm(wannier_table),
    )
    own = parts[0].reshape(ROWS, LANES)
    others = [
        lax.ppermute(parts[s].reshape(ROWS, LANES), "rp", [(j, j ^ s) for j in range(N_RP)])
        for s in range(1, N_RP)
    ]

    wanted = lax.all_to_all(requests, "re", split_axis=0, concat_axis=0, tiled=True)

    spread = pl.pallas_call(
        sum_kernel,
        in_specs=[vmem] * N_RP,
        out_specs=hbm,
        out_shape=pltpu.HBM((N_RE, PACK, LANES), BF),
        scratch_shapes=[pltpu.VMEM((ROWS, LANES), BF), pltpu.SemaphoreType.DMA((N_RE,))],
        compiler_params=params(8),
        name="sum",
    )(own, *others)
    packed = pl.pallas_call(
        lookup_kernel,
        grid=(1,),
        in_specs=[
            pl.BlockSpec(memory_space=pltpu.HBM),
            pl.BlockSpec(memory_space=pltpu.VMEM),
            pl.BlockSpec(memory_space=pltpu.VMEM),
        ],
        out_specs=pl.BlockSpec((N_RE, CAP, LANES), lambda i: (0, ROWS // CAP, 0)),
        out_shape=pltpu.HBM((N_RE, PACK, LANES), BF),
        input_output_aliases={0: 0},
        compiler_params=params(8),
        name="lookup",
    )(spread, wanted, rotations)
    gathered = lax.all_to_all(packed, "re", split_axis=0, concat_axis=0, tiled=True)

    def phase_tiles(coords, space):
        tiles = coords.shape[1] // LANES
        return pl.pallas_call(
            phase_kernel,
            out_shape=space((tiles, RE, 2 * LANES), BF),
            compiler_params=params(16),
            name="phase",
        )(in_hbm(re_coords), in_hbm(coords))

    first = phase_tiles(k_coords[:, : FIRST * LANES], pltpu.VMEM)
    later = phase_tiles(k_coords[:, FIRST * LANES :], pltpu.HBM)

    near = pl.pallas_call(
        near_kernel,
        in_specs=[vmem],
        out_shape=pltpu.VMEM((3 * SIZE, K), F32),
        compiler_params=params(8),
        name="near",
    )(rotations)
    slots, first, later, near = lax.optimization_barrier((slots, first, later, near))
    far = pl.pallas_call(
        far_kernel,
        in_specs=[vmem, vmem],
        out_shape=jax.ShapeDtypeStruct((LANES, K), BF),
        compiler_params=params(16),
        name="far",
    )(slots, gathered)
    mate = lax.ppermute(far, "rp", [(j, j ^ 1) for j in range(N_RP)])
    coupling = pl.pallas_call(
        couple_kernel,
        in_specs=[vmem, hbm, vmem],
        out_shape=pltpu.VMEM((TILES, Q * M_LOCAL, 3 * SIZE, LANES), F32),
        scratch_shapes=[
            pltpu.VMEM((TILES - FIRST, RE, 2 * LANES), BF),
            pltpu.VMEM((Q * M_LOCAL, LANES, RE), BF),
            pltpu.SemaphoreType.DMA((TILES - FIRST,)),
        ],
        compiler_params=params(16),
        name="couple",
    )(first, in_hbm(later), gathered)
    result = pl.pallas_call(
        final_kernel,
        in_specs=[smem(), vmem, vmem, vmem, vmem],
        out_specs=hbm,
        out_shape=jax.ShapeDtypeStruct((Q * M_LOCAL, 2, SIZE, K), BF),
        scratch_shapes=[
            pltpu.VMEM((Q, 3 * SIZE, K), F32),
            pltpu.VMEM((TILES, Q * M_LOCAL, 2, SIZE, LANES), BF),
            pltpu.SemaphoreType.DMA((TILES, Q)),
        ],
        compiler_params=params(16),
        name="final",
    )(rank, near, far, mate, coupling)
    return result.reshape(Q, M_LOCAL, 2, NB * NB, K)


def solution(mesh):
    in_specs = (
        P("re", "rp", None),
        P(),
        P(),
        P(None, "rp"),
        P(),
        P(None, "re"),
        P("re", None),
        P(None, "re", None),
        P(None, "re"),
    )
    out_specs = P(None, "rp", None, None, "re")
    return jax.shard_map(local, mesh=mesh, in_specs=in_specs, out_specs=out_specs, check_vma=False)
```
